128 devices in a mesh: image: 4 (over y), token: 32 (over z, x, core).
Axes of the slice: x: 4, y: 4, z: 4, core: 2. Of those that a mesh axis runs over, the one named last changes fastest.
Arguments:
- hidden: bfloat16 [2, 4, 4096, 3072], P(None, 'image', 'token'), may hold values from -6 to 6
- key_cache: bfloat16 [2, 4, 4096, 1536], P(None, 'image', 'token')
- value_cache: bfloat16 [2, 4, 4096, 1536], P(None, 'image', 'token'), may hold values from -6 to 6
- cached_out: bfloat16 [4, 4096, 1536], P('image', 'token'), may hold values from -6 to 6
- w_query: bfloat16 [3072, 1536], P('image'), may hold values from -0.109375 to 0.109375
- guide: float32 [4], P('image'), may hold values from 1.5 to 4
- masked_tiles: int32 [4, 8], P('image'), may hold values from 0 to 31, as said below
- mask_count: int32 [4], P('image'), may hold values from 4 to 8, as said below
Outputs:
- edited: bfloat16 [4, 4096, 1536], P('image', 'token')
The draws below stay inside these ranges and needn't reach their ends.
Inputs may be any that keep to these rules, and one draw needn't show every extreme that they name: `masked_tiles`: in each image the first mask_count entries are distinct tiles; later entries are tiles too. `mask_count`: some image of every draw has exactly 8 masked tiles.
All inputs are finite; a program needn't handle non-finite values.
Results may differ from the reference program's by a relative error of at most 0.011.
The reference program's roundings to bfloat16 on the way count: a program that leaves them out, or rounds other values in their place, can miss the bound.
Values may be sent and summed in bfloat16 or wider, within the bound.
A program may use at most 128 MiB of HBM per device.

```python
import math
import jax
import jax.numpy as jnp
from jax import lax

D = 3072
HD = 128
HEADS = 12
INNER = 1536
TILE = 128
L = 4096
IMAGE_COUNT = 4
MASK_MOST = 8


def mask_layout(key):
    starting_key = jax.random.fold_in(key, 17)
    image_keys = jax.random.split(jax.random.fold_in(starting_key, 1), IMAGE_COUNT)

    def one_image(image_key):
        return jax.random.permutation(image_key, L // TILE)[:MASK_MOST].astype(jnp.int32)
    tiles = jax.vmap(one_image)(image_keys).astype(jnp.int32)
    counts = jax.random.randint(jax.random.fold_in(starting_key, 2), (IMAGE_COUNT,), (MASK_MOST + 1) // 2, MASK_MOST + 1).astype(jnp.int32)
    fullest = jax.random.randint(jax.random.fold_in(starting_key, 3), (), 0, IMAGE_COUNT)
    counts = jnp.where(jnp.arange(IMAGE_COUNT) == fullest, MASK_MOST, counts).astype(jnp.int32)
    return (tiles, counts)


def draw_masked_tiles(key, part):
    tiles, counts = mask_layout(key)
    return tiles


def draw_mask_count(key, part):
    tiles, counts = mask_layout(key)
    return counts


def draw_key_cache(key, part):
    shape = (2, IMAGE_COUNT, L, HEADS * HD)
    entries = jax.random.normal(jax.random.fold_in(key, 5), shape, jnp.float32)
    return entries.astype(jnp.bfloat16)


def level_of(rng, dims, cuts, smallest, high):
    loudness, own = 1.0, jax.random.fold_in(rng, 6)
    for dim, parts in cuts:
        heights = jnp.exp(jax.random.uniform(jax.random.fold_in(own, dim), (parts,), jnp.float32, smallest / len(cuts), high / len(cuts)))
        loudness = loudness * jnp.repeat(heights, dims[dim] // parts).reshape([-1 if axis == dim else 1 for axis in range(len(dims))])
    return loudness


def scatter_about(own_key, shape, scale, reach, pieces=(), held_as=jnp.bfloat16):
    level = level_of(own_key, shape, pieces, -0.22, 0.18) if pieces else 1.0
    array = jax.random.normal(own_key, shape, jnp.float32) * scale * level
    return jnp.minimum(jnp.maximum(array, -reach), reach).astype(held_as)


def setup_inputs(seed: int = 0) -> dict:
    key_of = jax.random.split(jax.random.key(seed), 9)
    return {
        "hidden": scatter_about(key_of[0], (2, IMAGE_COUNT, L, D), 1.0, 6.0, ((1, 4), (2, 32))),
        "key_cache": draw_key_cache(jax.random.fold_in(key_of[8], 71), 0),
        "value_cache": scatter_about(key_of[2], (2, IMAGE_COUNT, L, INNER), 1.0, 6.0, ((1, 4), (2, 32))),
        "cached_out": scatter_about(key_of[3], (IMAGE_COUNT, L, INNER), 1.0, 6.0, ((0, 4), (1, 32))),
        "w_query": scatter_about(key_of[4], (D, INNER), D ** -0.5, 0.109375, ((0, 4),)),
        "guide": jnp.clip(1.5 + 2.5 * jax.random.uniform(key_of[5], (IMAGE_COUNT,), jnp.float32) ** level_of(key_of[5], (IMAGE_COUNT,), ((0, 4),), -0.2, 0.2), 1.5, 4.0),
        "masked_tiles": draw_masked_tiles(jax.random.fold_in(key_of[8], 71), 0),
        "mask_count": draw_mask_count(jax.random.fold_in(key_of[8], 71), 0),
    }


def one_head(operands):
    head_queries, head_keys, head_values = operands
    scale_for_scores = 1.0 / math.sqrt(HD)
    logit_scores = jnp.einsum('tzh,tjh->tzj', head_queries.astype(jnp.float32), head_keys.astype(jnp.float32), precision=lax.Precision.HIGHEST) * scale_for_scores
    row_max = lax.optimization_barrier(jnp.max(logit_scores, axis=-1, keepdims=True))
    exp_scores = jnp.exp(logit_scores - row_max)
    row_total = lax.optimization_barrier(jnp.sum(exp_scores, axis=-1, keepdims=True))
    softmax_weights = (exp_scores / row_total).astype(jnp.bfloat16)
    return jnp.einsum('enj,ejh->enh', softmax_weights.astype(jnp.float32), head_values.astype(jnp.float32), precision=lax.Precision.HIGHEST)

def attend(queries, key_block, value_block):
    rows_all = queries.shape[1]
    query_heads = jnp.moveaxis(queries.reshape(2, rows_all, HEADS, HD), 2, 0)
    key_heads = jnp.moveaxis(key_block.reshape(2, L, HEADS, HD), 2, 0)
    value_heads = jnp.moveaxis(value_block.reshape(2, L, HEADS, HD), 2, 0)
    attended = lax.map(one_head, (query_heads, key_heads, value_heads))
    return jnp.moveaxis(attended, 0, 2).reshape(2, rows_all, HEADS * HD)

def reference(hidden, key_cache, value_cache, cached_out, w_query, guide, masked_tiles, mask_count):
    edited_all = []
    for image_index in range(IMAGE_COUNT):
        image_hidden = hidden[:, image_index]
        starts = (masked_tiles[image_index] * TILE).astype(jnp.int32)

        def take_tile(first_row):
            return lax.dynamic_slice_in_dim(image_hidden, first_row, TILE, 1)
        tile_rows = jax.vmap(take_tile)(starts)
        tile_rows = jnp.moveaxis(tile_rows, 0, 1).reshape(2 * MASK_MOST * TILE, D)
        queries = jnp.dot(tile_rows, w_query, preferred_element_type=jnp.float32).astype(jnp.bfloat16)
        queries = queries.reshape(2, MASK_MOST * TILE, HEADS * HD)
        attended = attend(queries, key_cache[:, image_index], value_cache[:, image_index])
        guided = attended[1] + guide[image_index] * (attended[0] - attended[1])
        guided = guided.astype(jnp.bfloat16).reshape(MASK_MOST, TILE, HEADS * HD)
        field_out = cached_out[image_index]
        for slot_index in range(MASK_MOST):
            first_row = (masked_tiles[image_index, slot_index] * TILE).astype(jnp.int32)
            previous = lax.dynamic_slice_in_dim(field_out, first_row, TILE, 0)
            chosen = jnp.where(slot_index < mask_count[image_index], guided[slot_index], previous)
            field_out = lax.dynamic_update_slice_in_dim(field_out, chosen, first_row, 0)
        edited_all.append(field_out)
    return jnp.stack(edited_all)
```

```python
import functools
import math

import jax
import jax.numpy as jnp
from jax import lax
from jax.experimental import pallas as pl
from jax.experimental.pallas import tpu as pltpu
from jax.sharding import PartitionSpec as P

HD = 128
TILE = 128
SIDE = 4
MESH = pl.DeviceIdType.MESH
LOG2E = 1.4426950408889634


def head_chip(head):
    row = head // (SIDE - 1)
    col = (row + 1 + head % (SIDE - 1)) % SIDE
    return row * SIDE + col


def kernel(
    tiles_ref,
    count_ref,
    guide_ref,
    hidden_ref,
    key_ref,
    value_ref,
    w_ref,
    out_ref,
    hid,
    wbuf,
    acc,
    qsend,
    qbuf,
    kbuf,
    vbuf,
    score,
    attended,
    other,
    guided,
    osend,
    local_sem,
    hid_sem,
    w_send,
    w_recv,
    kv_send,
    kv_recv,
    q_send,
    q_recv,
    x_sem,
    o_send,
    o_recv,
):
    image = lax.axis_index("image")
    token = lax.axis_index("token")
    images = hidden_ref.shape[3] // w_ref.shape[0]
    core = lax.rem(token, 2)
    chip = token // 2
    partner = token + 1 - 2 * core
    row = chip // SIDE
    col = lax.rem(chip, SIDE)
    turn = lax.rem(col - row - 1 + 2 * SIDE, SIDE)
    has_head = turn < SIDE - 1
    my_head = jnp.minimum(row * (SIDE - 1) + turn, 11)
    token_count = 2 * SIDE * SIDE
    heads = key_ref.shape[3] // HD
    half_heads = heads // 2
    depth = w_ref.shape[0]
    half_cols = w_ref.shape[1] // 2
    slots = tiles_ref.shape[1]
    up = lax.rem(image + 1, images)
    down = lax.rem(image + images - 1, images)

    my_cols = pl.ds(pl.multiple_of(core * half_cols, 128), half_cols)
    w_own = pltpu.make_async_copy(w_ref.at[:, my_cols], wbuf.at[0], local_sem.at[0])
    w_own.start()
    hid_own = pltpu.make_async_copy(hidden_ref.at[:, 0], hid.at[:, core], local_sem.at[1])
    hid_own.start()

    barrier = pltpu.get_barrier_semaphore()

    @pl.loop(1, token_count)
    def _(step):
        peer = lax.rem(token + step, token_count)
        pl.semaphore_signal(barrier, inc=1, device_id=(image, peer), device_id_type=MESH)

    for near in (up, down):
        pl.semaphore_signal(barrier, inc=1, device_id=(near, token), device_id_type=MESH)
    pl.semaphore_wait(barrier, token_count - 1 + 2)

    half = depth // 2
    first, second = pl.ds(0, half), pl.ds(half, half)

    def w_copy(index, src, slot, rows, near):
        return pltpu.make_async_remote_copy(
            src_ref=src,
            dst_ref=wbuf.at[slot, rows],
            send_sem=w_send.at[index],
            recv_sem=w_recv.at[index],
            device_id=(near, token),
            device_id_type=MESH,
        )

    up_first = w_copy(0, w_ref.at[first, my_cols], 1, first, up)
    down_second = w_copy(1, w_ref.at[second, my_cols], 2, second, down)
    up_second = w_copy(2, w_ref.at[second, my_cols], 1, second, up)
    down_first = w_copy(3, w_ref.at[first, my_cols], 2, first, down)
    up_relay = w_copy(4, wbuf.at[1, first], 3, first, up)
    down_relay = w_copy(5, wbuf.at[2, second], 3, second, down)
    for copy in (up_first, down_second, up_second, down_first):
        copy.start()

    hid_out = pltpu.make_async_remote_copy(
        src_ref=hidden_ref.at[:, 0],
        dst_ref=hid.at[:, core],
        send_sem=hid_sem.at[0],
        recv_sem=hid_sem.at[1],
        device_id=(image, partner),
        device_id_type=MESH,
    )
    hid_out.start()

    def kv_pair(step):
        branch = lax.rem(step, 2)
        head = lax.rem(my_head + step // 2, heads)
        target = head_chip(head) * 2 + branch
        lanes = pl.ds(pl.multiple_of(head * HD, HD), HD)
        pairs = (
            (key_ref.at[branch, 0, :, lanes], kbuf.at[token], 0),
            (value_ref.at[branch, 0, :, lanes], vbuf.at[token], 1),
        )
        return target, pairs

    def kv_remote(step, target, src, dst, kind):
        return pltpu.make_async_remote_copy(
            src_ref=src,
            dst_ref=dst,
            send_sem=kv_send.at[kind, step],
            recv_sem=kv_recv.at[kind],
            device_id=(image, target),
            device_id_type=MESH,
        )

    @pl.loop(0, 2 * heads)
    def _(step):
        target, pairs = kv_pair(step)

        @pl.when(target != token)
        def _():
            for src, dst, kind in pairs:
                kv_remote(step, target, src, dst, kind).start()

        @pl.when(target == token)
        def _():
            for src, dst, kind in pairs:
                pltpu.make_async_copy(src, dst, kv_recv.at[kind]).start()

    rows_all = 4 * TILE
    width = 256

    def project(slot, owner, start, size, is_first):
        features = pl.ds(pl.multiple_of(owner * depth + start, 128), size)

        @pl.loop(0, half_cols // width)
        def _(step):
            cols = pl.ds(pl.multiple_of(step * width, width), width)
            part = jnp.dot(
                hid[:, :, :, features].reshape(rows_all, size),
                wbuf[slot, pl.ds(start, size), cols],
                preferred_element_type=jnp.float32,
            )
            if is_first:
                acc[:, cols] = part
            else:
                acc[:, cols] += part

    far = lax.rem(image + 2, images)
    w_own.wait()
    hid_own.wait()
    hid_out.wait_recv()
    project(0, image, 0, depth, True)
    up_first.wait_recv()
    up_relay.start()
    down_second.wait_recv()
    down_relay.start()
    project(1, down, 0, half, False)
    project(2, up, half, half, False)
    up_second.wait_recv()
    project(1, down, half, half, False)
    down_first.wait_recv()
    project(2, up, 0, half, False)
    up_relay.wait_recv()
    project(3, far, 0, half, False)
    down_relay.wait_recv()
    project(3, far, half, half, False)

    for head in range(half_heads):
        block = acc[:, head * HD : (head + 1) * HD].astype(jnp.bfloat16)
        qsend[:, head] = block.reshape(2, 2, TILE, HD)

    def q_where(step):
        branch = lax.rem(step, 2)
        local_head = lax.rem(my_head + step // 2, half_heads)
        target = head_chip(core * half_heads + local_head) * 2 + branch
        return target, qsend.at[branch, local_head], qbuf.at[pl.ds(chip * 2, 2)]

    def q_remote(step):
        target, src, dst = q_where(step)
        return pltpu.make_async_remote_copy(
            src_ref=src,
            dst_ref=dst,
            send_sem=q_send.at[step],
            recv_sem=q_recv,
            device_id=(image, target),
            device_id_type=MESH,
        )

    @pl.loop(0, 2 * half_heads)
    def _(step):
        target, src, dst = q_where(step)

        @pl.when(target != token)
        def _():
            q_remote(step).start()

        @pl.when(target == token)
        def _():
            pltpu.make_async_copy(src, dst, q_recv).start()

    share = TILE // 2
    mine_rows = pl.ds(pl.multiple_of(core * share, share), share)
    sent_rows = pl.ds(pl.multiple_of((1 - core) * share, share), share)
    exchange = pltpu.make_async_remote_copy(
        src_ref=attended.at[:, sent_rows],
        dst_ref=other,
        send_sem=x_sem.at[0],
        recv_sem=x_sem.at[1],
        device_id=(image, partner),
        device_id_type=MESH,
    )

    def o_where(target):
        lanes = pl.ds(pl.multiple_of(my_head * HD, HD), HD)
        return osend.at[target], out_ref.at[mine_rows, lanes]

    def o_remote(target):
        src, dst = o_where(target)
        return pltpu.make_async_remote_copy(
            src_ref=src,
            dst_ref=dst,
            send_sem=o_send.at[target],
            recv_sem=o_recv,
            device_id=(image, target),
            device_id_type=MESH,
        )

    @pl.when(has_head)
    def _():
        pltpu.make_async_copy(kbuf, kbuf, kv_recv.at[0]).wait()
        pltpu.make_async_copy(vbuf, vbuf, kv_recv.at[1]).wait()
        pltpu.make_async_copy(qbuf, qbuf, q_recv).wait()
        factor = LOG2E / math.sqrt(HD)
        span = 8
        chunk = span * TILE
        chunks = token_count // span

        @pl.loop(0, slots // 2)
        def _(pair):
            query = jnp.concatenate(
                [qbuf[tiles_ref[0, 2 * pair]], qbuf[tiles_ref[0, 2 * pair + 1]]], axis=0
            )
            peak = jnp.full((2 * TILE, 128), -jnp.inf, jnp.float32)
            for part in range(chunks):
                keys = kbuf[part * span : (part + 1) * span].reshape(chunk, HD)
                logits = lax.dot_general(
                    query, keys, (((1,), (1,)), ((), ())), preferred_element_type=jnp.float32
                )
                score[:, part * chunk : (part + 1) * chunk] = logits
                for piece in range(span):
                    peak = jnp.maximum(peak, logits[:, piece * 128 : (piece + 1) * 128])
            top = jnp.max(peak, axis=-1, keepdims=True) * factor
            total = jnp.zeros((2 * TILE, 128), jnp.float32)
            summed = jnp.zeros((2 * TILE, HD), jnp.float32)
            for part in range(chunks):
                values = vbuf[part * span : (part + 1) * span].reshape(chunk, HD)
                weight = jnp.exp2(score[:, part * chunk : (part + 1) * chunk] * factor - top)
                for piece in range(span):
                    total = total + weight[:, piece * 128 : (piece + 1) * 128]
                summed = summed + jnp.dot(
                    weight.astype(jnp.bfloat16), values, preferred_element_type=jnp.float32
                )
            summed = summed / jnp.sum(total, axis=-1, keepdims=True)
            attended[pl.ds(2 * pair, 2)] = summed.reshape(2, TILE, HD)

        exchange.start()
        exchange.wait_recv()
        scale = guide_ref[0]
        mine = attended[:, mine_rows]
        theirs = other[...]
        cond = jnp.where(core == 0, mine, theirs)
        uncond = jnp.where(core == 0, theirs, mine)
        guided[...] = (uncond + scale * (cond - uncond)).astype(jnp.bfloat16)

        @pl.loop(0, token_count)
        def _(target):
            slot = jnp.int32(0)
            for j in range(slots):
                slot = jnp.where(
                    (tiles_ref[0, j] == target) & (count_ref[0] > j), jnp.int32(j), slot
                )
            osend[target] = guided[slot]

        @pl.loop(0, token_count)
        def _(step):
            target = lax.rem(token + step, token_count)

            @pl.when(target != token)
            def _():
                o_remote(target).start()

            @pl.when(target == token)
            def _():
                src, dst = o_where(target)
                pltpu.make_async_copy(src, dst, o_recv).start()

    for copy in (up_first, down_second, up_second, down_first, up_relay, down_relay, hid_out):
        copy.wait_send()

    @pl.loop(0, 2 * heads)
    def _(step):
        target, pairs = kv_pair(step)

        @pl.when(target != token)
        def _():
            for src, dst, kind in pairs:
                kv_remote(step, target, src, dst, kind).wait_send()

    @pl.loop(0, 2 * half_heads)
    def _(step):
        target, _, _ = q_where(step)

        @pl.when(target != token)
        def _():
            q_remote(step).wait_send()

    @pl.when(has_head)
    def _():
        exchange.wait_send()

        @pl.loop(0, token_count)
        def _(target):
            @pl.when(target != token)
            def _():
                o_remote(target).wait_send()

    pltpu.make_async_copy(out_ref, out_ref, o_recv).wait()


def attend(hidden, key_cache, value_cache, w_query, guide, masked_tiles, mask_count):
    tokens = 2 * SIDE * SIDE
    inner = key_cache.shape[3]
    heads = inner // HD
    slots = masked_tiles.shape[1]
    width = hidden.shape[3]
    images = width // w_query.shape[0]
    dma = pltpu.SemaphoreType.DMA
    return pl.pallas_call(
        kernel,
        out_shape=jax.ShapeDtypeStruct((TILE, inner), jnp.bfloat16),
        in_specs=[pl.BlockSpec(memory_space=pltpu.SMEM)] * 3
        + [pl.BlockSpec(memory_space=pl.ANY)] * 4,
        out_specs=pl.BlockSpec(memory_space=pltpu.VMEM),
        scratch_shapes=[
            pltpu.VMEM((2, 2, TILE, width), jnp.bfloat16),
            pltpu.VMEM((images, w_query.shape[0], inner // 2), jnp.bfloat16),
            pltpu.VMEM((4 * TILE, inner // 2), jnp.float32),
            pltpu.VMEM((2, heads // 2, 2, TILE, HD), jnp.bfloat16),
            pltpu.VMEM((tokens, TILE, HD), jnp.bfloat16),
            pltpu.VMEM((tokens, TILE, HD), jnp.bfloat16),
            pltpu.VMEM((tokens, TILE, HD), jnp.bfloat16),
            pltpu.VMEM((2 * TILE, tokens * TILE), jnp.float32),
            pltpu.VMEM((slots, TILE, HD), jnp.float32),
            pltpu.VMEM((slots, TILE // 2, HD), jnp.float32),
            pltpu.VMEM((slots, TILE // 2, HD), jnp.bfloat16),
            pltpu.VMEM((tokens, TILE // 2, HD), jnp.bfloat16),
            dma((2,)),
            dma((2,)),
            dma((6,)),
            dma((6,)),
            dma((2, 2 * heads)),
            dma((2,)),
            dma((heads,)),
            dma,
            dma((2,)),
            dma((tokens,)),
            dma,
        ],
        compiler_params=pltpu.CompilerParams(
            collective_id=0, has_side_effects=True, vmem_limit_bytes=60 * 1024 * 1024
        ),
    )(masked_tiles, mask_count, guide, hidden, key_cache, value_cache, w_query)


def body(hidden, key_cache, value_cache, cached_out, w_query, guide, masked_tiles, mask_count):
    rows = attend(hidden, key_cache, value_cache, w_query, guide, masked_tiles, mask_count)
    token = lax.axis_index("token")
    used = jnp.arange(masked_tiles.shape[1], dtype=jnp.int32) < mask_count[0]
    pasted = jnp.any((masked_tiles[0] == token) & used)
    return jnp.where(pasted, rows[None], cached_out)


def solution(mesh):
    return jax.shard_map(
        body,
        mesh=mesh,
        in_specs=(
            P(None, "image", "token", None),
            P(None, "image", "token", None),
            P(None, "image", "token", None),
            P("image", "token", None),
            P("image", None),
            P("image"),
            P("image", None),
            P("image"),
        ),
        out_specs=P("image", "token", None),
        check_vma=False,
    )
```

```python
import functools
import math

import jax
import jax.numpy as jnp
from jax import lax
from jax.experimental import pallas as pl
from jax.experimental.pallas import tpu as pltpu
from jax.sharding import PartitionSpec as P

HD = 128
TILE = 128
SIDE = 4
STAGES = 4
PARTS = 3
MESH = pl.DeviceIdType.MESH
LOG2E = 1.4426950408889634


def head_of(row, col):
    turn = lax.rem(col - row - 1 + 2 * SIDE, SIDE)
    last = SIDE - 2
    return row * (SIDE - 1) + jnp.minimum(turn, last), turn <= last


def offset_chip(row, col, step):
    turn = step // SIDE
    to_row = lax.rem(row + 2 * turn + step, SIDE)
    to_col = lax.rem(col + 3 * turn + step, SIDE)
    return to_row, to_col


def kernel(
    tiles_ref,
    count_ref,
    guide_ref,
    hidden_ref,
    key_ref,
    value_ref,
    w_ref,
    out_ref,
    hid,
    wbuf,
    acc,
    qsend,
    qbuf,
    qnow,
    kbuf,
    vbuf,
    score,
    attended,
    other,
    guided,
    osend,
    slot_of,
    local_sem,
    hid_sem,
    w_send,
    w_recv,
    kv_send,
    kv_recv,
    q_send,
    q_recv,
    x_send,
    x_recv,
    o_send,
    o_recv,
):
    image = lax.axis_index("image")
    token = lax.axis_index("token")
    images = hidden_ref.shape[3] // w_ref.shape[0]
    core = lax.rem(token, 2)
    chip = token // 2
    partner = token + 1 - 2 * core
    row = chip // SIDE
    col = lax.rem(chip, SIDE)
    my_head, has_head = head_of(row, col)
    odd = lax.rem(col, 2)
    right = (row * SIDE + lax.rem(col + 1, SIDE)) * 2 + core
    left = (row * SIDE + lax.rem(col + SIDE - 1, SIDE)) * 2 + core
    token_count = 2 * SIDE * SIDE
    heads = key_ref.shape[3] // HD
    half_heads = heads // 2
    depth = w_ref.shape[0]
    half_cols = w_ref.shape[1] // 2
    slots = tiles_ref.shape[1]
    up = lax.rem(image + 1, images)
    down = lax.rem(image + images - 1, images)

    my_cols = pl.ds(pl.multiple_of(core * half_cols, 128), half_cols)
    w_own = pltpu.make_async_copy(w_ref.at[:, my_cols], wbuf.at[0], local_sem.at[0])
    w_own.start()
    hid_own = pltpu.make_async_copy(hidden_ref.at[:, 0], hid.at[:, core], local_sem.at[1])
    hid_own.start()

    barrier = pltpu.get_barrier_semaphore()

    @pl.loop(1, token_count)
    def _(step):
        peer = lax.rem(token + step, token_count)
        pl.semaphore_signal(barrier, inc=1, device_id=(image, peer), device_id_type=MESH)

    for near in (up, down):
        pl.semaphore_signal(barrier, inc=1, device_id=(near, token), device_id_type=MESH)
    pl.semaphore_wait(barrier, token_count - 1 + 2)

    half = depth // 2
    piece = half // PARTS
    early_1, early_2 = 1 - odd, odd

    def w_rows(part, k):
        return pl.ds(pl.multiple_of(part * half + k * piece, 128), piece)

    def w_copy(index, src, slot, part, k, to_image, to_token):
        return pltpu.make_async_remote_copy(
            src_ref=src,
            dst_ref=wbuf.at[slot, w_rows(part, k)],
            send_sem=w_send.at[index, k],
            recv_sem=w_recv.at[slot - 1, part, k],
            device_id=(to_image, to_token),
            device_id_type=MESH,
        )

    def w_direct(index, slot, part, k):
        near = up if slot == 1 else down
        return w_copy(index, w_ref.at[w_rows(part, k), my_cols], slot, part, k, near, token)

    def w_pass(index, slot, part, k, new_slot, to_image, to_token):
        src = wbuf.at[slot, w_rows(part, k)]
        return w_copy(index, src, new_slot, part, k, to_image, to_token)

    def w_wait(slot, part, k):
        dst = wbuf.at[slot, w_rows(part, k)]
        pltpu.make_async_copy(dst, dst, w_recv.at[slot - 1, part, k]).wait()

    def direct_early(k):
        return w_direct(0, 1, early_1, k), w_direct(1, 2, early_2, k)

    def direct_late(k):
        return w_direct(2, 1, 0, k), w_direct(3, 2, 1, k)

    def pass_early(k):
        to_1 = jnp.where(odd == 1, token, right)
        to_2 = jnp.where(odd == 1, token, left)
        return (
            w_pass(4, 1, early_1, k, 1 + 2 * odd, jnp.where(odd == 1, up, image), to_1),
            w_pass(5, 2, early_2, k, 2 + odd, jnp.where(odd == 1, down, image), to_2),
        )

    def pass_late(k):
        return w_pass(2, 3, 0, k, 3, image, right), w_pass(3, 3, 1, k, 3, image, left)

    for k in range(PARTS):
        for copy in direct_early(k):
            copy.start()

    @pl.when(odd == 0)
    def _():
        for k in range(PARTS):
            for copy in direct_late(k):
                copy.start()

    hid_out = pltpu.make_async_remote_copy(
        src_ref=hidden_ref.at[:, 0],
        dst_ref=hid.at[:, core],
        send_sem=hid_sem.at[0],
        recv_sem=hid_sem.at[1],
        device_id=(image, partner),
        device_id_type=MESH,
    )
    hid_out.start()

    def kv_pair(step):
        branch = lax.rem(step, 2)
        to_row, to_col = offset_chip(row, col, step // 2)
        head, there = head_of(to_row, to_col)
        target = (to_row * SIDE + to_col) * 2 + branch
        lanes = pl.ds(pl.multiple_of(head * HD, HD), HD)
        pairs = (
            (key_ref.at[branch, 0, :, lanes], kbuf.at[token], 0),
            (value_ref.at[branch, 0, :, lanes], vbuf.at[token], 1),
        )
        return target, there, pairs

    def kv_remote(step, target, src, dst, kind):
        return pltpu.make_async_remote_copy(
            src_ref=src,
            dst_ref=dst,
            send_sem=kv_send.at[kind, step],
            recv_sem=kv_recv.at[kind],
            device_id=(image, target),
            device_id_type=MESH,
        )

    @pl.loop(0, token_count)
    def _(step):
        target, there, pairs = kv_pair(step)

        @pl.when(there & (target != token))
        def _():
            for src, dst, kind in pairs:
                kv_remote(step, target, src, dst, kind).start()

        @pl.when(there & (target == token))
        def _():
            for src, dst, kind in pairs:
                pltpu.make_async_copy(src, dst, kv_recv.at[kind]).start()

    @pl.loop(0, token_count)
    def _(tile):
        slot = jnp.int32(0)
        for j in range(slots):
            hit = (tiles_ref[0, j] == tile) & (count_ref[0] > j)
            slot = jnp.where(hit, jnp.int32(j), slot)
        slot_of[tile] = slot

    rows_all = 4 * TILE
    width = 256

    def project(slot, owner, start, size, is_first):
        features = pl.ds(pl.multiple_of(owner * depth + start, 128), size)
        w_part = pl.ds(pl.multiple_of(start, 128), size)

        @pl.loop(0, half_cols // width)
        def _(step):
            cols = pl.ds(pl.multiple_of(step * width, width), width)
            part = jnp.dot(
                hid[:, :, :, features].reshape(rows_all, size),
                wbuf[slot, w_part, cols],
                preferred_element_type=jnp.float32,
            ).reshape(2, 2, TILE, width)
            if is_first:
                acc[:, :, :, cols] = part
            else:
                acc[:, :, :, cols] += part

    far = lax.rem(image + 2, images)
    w_own.wait()
    hid_own.wait()
    hid_out.wait_recv()
    project(0, image, 0, depth, True)
    for k in range(PARTS):
        first, second = pass_early(k)
        w_wait(1, early_1, k)
        first.start()
        w_wait(2, early_2, k)
        second.start()
    project(1, down, early_1 * half, half, False)
    project(2, up, early_2 * half, half, False)

    @pl.when(odd == 1)
    def _():
        for k in range(PARTS):
            first, second = pass_late(k)
            w_wait(3, 0, k)
            first.start()
            w_wait(3, 1, k)
            second.start()

    for k in range(PARTS):
        w_wait(1, 1 - early_1, k)
    project(1, down, (1 - early_1) * half, half, False)
    for k in range(PARTS):
        w_wait(2, 1 - early_2, k)
    project(2, up, (1 - early_2) * half, half, False)

    @pl.when(odd == 0)
    def _():
        for k in range(PARTS):
            w_wait(3, 0, k)
            w_wait(3, 1, k)

    project(3, far, 0, depth, False)

    rows = TILE // STAGES

    def q_where(stage, step):
        branch = lax.rem(step, 2)
        to_row, to_col = offset_chip(row, col, step // 2)
        head, there = head_of(to_row, to_col)
        there = there & (head // half_heads == core)
        target = (to_row * SIDE + to_col) * 2 + branch
        src = qsend.at[stage, branch, lax.rem(head, half_heads)]
        return target, there, src, qbuf.at[stage, pl.ds(chip * 2, 2)]

    def q_remote(stage, step):
        target, _, src, dst = q_where(stage, step)
        return pltpu.make_async_remote_copy(
            src_ref=src,
            dst_ref=dst,
            send_sem=q_send.at[stage, step],
            recv_sem=q_recv.at[stage],
            device_id=(image, target),
            device_id_type=MESH,
        )

    for stage in range(STAGES):
        for head in range(half_heads):
            block = acc[:, :, stage * rows : (stage + 1) * rows, head * HD : (head + 1) * HD]
            qsend[stage, :, head] = block.astype(jnp.bfloat16)

        @pl.loop(0, token_count)
        def _(step):
            target, there, src, dst = q_where(stage, step)

            @pl.when(there & (target != token))
            def _():
                q_remote(stage, step).start()

            @pl.when(there & (target == token))
            def _():
                pltpu.make_async_copy(src, dst, q_recv.at[stage]).start()

    share = rows // 2
    mine_rows = pl.ds(pl.multiple_of(core * share, share), share)
    sent_rows = pl.ds(pl.multiple_of((1 - core) * share, share), share)
    factor = LOG2E / math.sqrt(HD)
    span = 8
    chunk = span * TILE
    chunks = token_count // span
    height = slots * rows

    def exchange(stage):
        return pltpu.make_async_remote_copy(
            src_ref=attended.at[stage, :, sent_rows],
            dst_ref=other.at[stage],
            send_sem=x_send.at[stage],
            recv_sem=x_recv.at[stage],
            device_id=(image, partner),
            device_id_type=MESH,
        )

    def o_where(stage, target):
        lanes = pl.ds(pl.multiple_of(my_head * HD, HD), HD)
        put = pl.ds(pl.multiple_of(stage * rows + core * share, share), share)
        return osend.at[stage, target], out_ref.at[put, lanes]

    def o_remote(stage, target):
        src, dst = o_where(stage, target)
        return pltpu.make_async_remote_copy(
            src_ref=src,
            dst_ref=dst,
            send_sem=o_send.at[stage, target],
            recv_sem=o_recv,
            device_id=(image, target),
            device_id_type=MESH,
        )

    def attention(stage):
        qnow[...] = qbuf[stage]
        query = jnp.concatenate([qnow[tiles_ref[0, j]] for j in range(slots)], axis=0)
        peak = jnp.full((height, 128), -jnp.inf, jnp.float32)
        for part in range(chunks):
            keys = kbuf[part * span : (part + 1) * span].reshape(chunk, HD)
            logits = lax.dot_general(
                query, keys, (((1,), (1,)), ((), ())), preferred_element_type=jnp.float32
            )
            score[:, part * chunk : (part + 1) * chunk] = logits
            for lane in range(span):
                peak = jnp.maximum(peak, logits[:, lane * 128 : (lane + 1) * 128])
        top = jnp.max(peak, axis=-1, keepdims=True) * factor
        total = jnp.zeros((height, 128), jnp.float32)
        summed = jnp.zeros((height, HD), jnp.float32)
        for part in range(chunks):
            values = vbuf[part * span : (part + 1) * span].reshape(chunk, HD)
            weight = jnp.exp2(score[:, part * chunk : (part + 1) * chunk] * factor - top)
            for lane in range(span):
                total = total + weight[:, lane * 128 : (lane + 1) * 128]
            summed = summed + jnp.dot(
                weight.astype(jnp.bfloat16), values, preferred_element_type=jnp.float32
            )
        summed = summed / jnp.sum(total, axis=-1, keepdims=True)
        attended[stage] = summed.reshape(slots, rows, HD)

    def deliver(stage):
        exchange(stage).wait_recv()
        scale = guide_ref[0]
        mine = attended[stage, :, mine_rows]
        theirs = other[stage]
        cond = jnp.where(core == 0, mine, theirs)
        uncond = jnp.where(core == 0, theirs, mine)
        guided[stage] = (uncond + scale * (cond - uncond)).astype(jnp.bfloat16)

        @pl.loop(0, token_count)
        def _(tile):
            osend[stage, tile] = guided[stage, slot_of[tile]]

        @pl.loop(0, token_count)
        def _(step):
            to_row, to_col = offset_chip(row, col, step // 2)
            target = (to_row * SIDE + to_col) * 2 + lax.rem(step, 2)

            @pl.when(target != token)
            def _():
                o_remote(stage, target).start()

            @pl.when(target == token)
            def _():
                src, dst = o_where(stage, target)
                pltpu.make_async_copy(src, dst, o_recv).start()

    @pl.when(has_head)
    def _():
        pltpu.make_async_copy(kbuf, kbuf, kv_recv.at[0]).wait()
        pltpu.make_async_copy(vbuf, vbuf, kv_recv.at[1]).wait()

        @pl.loop(0, STAGES)
        def _(stage):
            pltpu.make_async_copy(qbuf.at[stage], qbuf.at[stage], q_recv.at[stage]).wait()
            attention(stage)
            exchange(stage).start()

            @pl.when(stage > 0)
            def _():
                deliver(stage - 1)

        deliver(STAGES - 1)

    hid_out.wait_send()
    for k in range(PARTS):
        for copy in direct_early(k) + pass_early(k):
            copy.wait_send()

    @pl.when(odd == 0)
    def _():
        for k in range(PARTS):
            for copy in direct_late(k):
                copy.wait_send()

    @pl.when(odd == 1)
    def _():
        for k in range(PARTS):
            for copy in pass_late(k):
                copy.wait_send()

    @pl.loop(0, token_count)
    def _(step):
        target, there, pairs = kv_pair(step)

        @pl.when(there & (target != token))
        def _():
            for src, dst, kind in pairs:
                kv_remote(step, target, src, dst, kind).wait_send()

    @pl.loop(0, STAGES)
    def _(stage):
        @pl.loop(0, token_count)
        def _(step):
            target, there, _, _ = q_where(stage, step)

            @pl.when(there & (target != token))
            def _():
                q_remote(stage, step).wait_send()

    @pl.when(has_head)
    def _():
        @pl.loop(0, STAGES)
        def _(stage):
            exchange(stage).wait_send()

            @pl.loop(0, token_count)
            def _(target):
                @pl.when(target != token)
                def _():
                    o_remote(stage, target).wait_send()

    pltpu.make_async_copy(out_ref, out_ref, o_recv).wait()


def attend(hidden, key_cache, value_cache, w_query, guide, masked_tiles, mask_count):
    tokens = 2 * SIDE * SIDE
    inner = key_cache.shape[3]
    heads = inner // HD
    slots = masked_tiles.shape[1]
    width = hidden.shape[3]
    images = width // w_query.shape[0]
    rows = TILE // STAGES
    dma = pltpu.SemaphoreType.DMA
    return pl.pallas_call(
        kernel,
        out_shape=jax.ShapeDtypeStruct((TILE, inner), jnp.bfloat16),
        in_specs=[pl.BlockSpec(memory_space=pltpu.SMEM)] * 3
        + [pl.BlockSpec(memory_space=pl.ANY)] * 4,
        out_specs=pl.BlockSpec(memory_space=pltpu.VMEM),
        scratch_shapes=[
            pltpu.VMEM((2, 2, TILE, width), jnp.bfloat16),
            pltpu.VMEM((images, w_query.shape[0], inner // 2), jnp.bfloat16),
            pltpu.VMEM((2, 2, TILE, inner // 2), jnp.float32),
            pltpu.VMEM((STAGES, 2, heads // 2, 2, rows, HD), jnp.bfloat16),
            pltpu.VMEM((STAGES, tokens, rows, HD), jnp.bfloat16),
            pltpu.VMEM((tokens, rows, HD), jnp.bfloat16),
            pltpu.VMEM((tokens, TILE, HD), jnp.bfloat16),
            pltpu.VMEM((tokens, TILE, HD), jnp.bfloat16),
            pltpu.VMEM((slots * rows, tokens * TILE), jnp.float32),
            pltpu.VMEM((STAGES, slots, rows, HD), jnp.float32),
            pltpu.VMEM((STAGES, slots, rows // 2, HD), jnp.float32),
            pltpu.VMEM((STAGES, slots, rows // 2, HD), jnp.bfloat16),
            pltpu.VMEM((STAGES, tokens, rows // 2, HD), jnp.bfloat16),
            pltpu.SMEM((tokens,), jnp.int32),
            dma((2,)),
            dma((2,)),
            dma((6, PARTS)),
            dma((images - 1, 2, PARTS)),
            dma((2, tokens)),
            dma((2,)),
            dma((STAGES, tokens)),
            dma((STAGES,)),
            dma((STAGES,)),
            dma((STAGES,)),
            dma((STAGES, tokens)),
            dma,
        ],
        compiler_params=pltpu.CompilerParams(
            collective_id=0, has_side_effects=True, vmem_limit_bytes=60 * 1024 * 1024
        ),
    )(masked_tiles, mask_count, guide, hidden, key_cache, value_cache, w_query)


def body(hidden, key_cache, value_cache, cached_out, w_query, guide, masked_tiles, mask_count):
    rows = attend(hidden, key_cache, value_cache, w_query, guide, masked_tiles, mask_count)
    token = lax.axis_index("token")
    used = jnp.arange(masked_tiles.shape[1], dtype=jnp.int32) < mask_count[0]
    pasted = jnp.any((masked_tiles[0] == token) & used)
    return jnp.where(pasted, rows[None], cached_out)


def solution(mesh):
    return jax.shard_map(
        body,
        mesh=mesh,
        in_specs=(
            P(None, "image", "token", None),
            P(None, "image", "token", None),
            P(None, "image", "token", None),
            P("image", "token", None),
            P("image", None),
            P("image"),
            P("image", None),
            P("image"),
        ),
        out_specs=P("image", "token", None),
        check_vma=False,
    )
```

```python
import functools
import math

import jax
import jax.numpy as jnp
from jax import lax
from jax.experimental import pallas as pl
from jax.experimental.pallas import tpu as pltpu
from jax.sharding import PartitionSpec as P

HD = 128
TILE = 128
SIDE = 4
STAGES = 4
PARTS = 6
MESH = pl.DeviceIdType.MESH
LOG2E = 1.4426950408889634


def head_of(row, col):
    turn = (col - row - 1) & (SIDE - 1)
    last = SIDE - 2
    return row * (SIDE - 1) + jnp.minimum(turn, last), turn <= last


OFFSETS = tuple(
    ((2 * (i // SIDE) + i) % SIDE, (3 * (i // SIDE) + i) % SIDE) for i in range(1, SIDE * SIDE)
)


def kernel(
    tiles_ref,
    count_ref,
    guide_ref,
    hidden_ref,
    key_ref,
    value_ref,
    w_ref,
    cached_ref,
    out_ref,
    hid,
    wbuf,
    acc,
    qsend,
    qbuf,
    qnow,
    kbuf,
    vbuf,
    score,
    attended,
    other,
    guided,
    osend,
    arrived,
    cached,
    slot_of,
    local_sem,
    hid_sem,
    w_send,
    w_recv,
    kv_send,
    kv_recv,
    q_send,
    q_recv,
    x_send,
    x_recv,
    o_send,
    o_recv,
):
    image = lax.axis_index("image")
    token = lax.axis_index("token")
    images = hidden_ref.shape[3] // w_ref.shape[0]
    core = token & 1
    chip = token >> 1
    partner = token ^ 1
    row = chip >> 2
    col = chip & (SIDE - 1)
    my_head, has_head = head_of(row, col)
    odd = col & 1
    right = (row * SIDE + ((col + 1) & (SIDE - 1))) * 2 + core
    left = (row * SIDE + ((col - 1) & (SIDE - 1))) * 2 + core
    token_count = 2 * SIDE * SIDE
    heads = key_ref.shape[3] // HD
    half_heads = heads // 2
    depth = w_ref.shape[0]
    half_cols = w_ref.shape[1] // 2
    slots = tiles_ref.shape[1]
    up = (image + 1) & (images - 1)
    down = (image - 1) & (images - 1)
    far = image ^ 2

    my_cols = pl.ds(pl.multiple_of(core * half_cols, 128), half_cols)
    w_own = pltpu.make_async_copy(w_ref.at[:, my_cols], wbuf.at[0], local_sem.at[0])
    w_own.start()
    hid_own = pltpu.make_async_copy(hidden_ref.at[:, 0], hid.at[:, core], local_sem.at[1])
    hid_own.start()
    cached_own = pltpu.make_async_copy(cached_ref.at[0], cached, local_sem.at[2])
    cached_own.start()

    barrier = pltpu.get_barrier_semaphore()

    for near in (up, down):
        pl.semaphore_signal(barrier, inc=1, device_id=(near, token), device_id_type=MESH)
    for step in range(1, token_count):
        peer = token ^ step
        pl.semaphore_signal(barrier, inc=1, device_id=(image, peer), device_id_type=MESH)
    pl.semaphore_wait(barrier, token_count - 1 + 2)

    half = depth // 2
    piece = half // PARTS
    early_1, early_2 = 1 - odd, odd

    def w_rows(part, k):
        return pl.ds(pl.multiple_of(part * half + k * piece, piece), piece)

    def w_copy(index, src, slot, part, k, to_image, to_token):
        return pltpu.make_async_remote_copy(
            src_ref=src,
            dst_ref=wbuf.at[slot, w_rows(part, k)],
            send_sem=w_send.at[index, k],
            recv_sem=w_recv.at[slot - 1, part, k],
            device_id=(to_image, to_token),
            device_id_type=MESH,
        )

    def w_direct(index, slot, part, k):
        near = up if slot == 1 else down
        return w_copy(index, w_ref.at[w_rows(part, k), my_cols], slot, part, k, near, token)

    def w_pass(index, slot, part, k, new_slot, to_image, to_token):
        src = wbuf.at[slot, w_rows(part, k)]
        return w_copy(index, src, new_slot, part, k, to_image, to_token)

    def w_wait(slot, part, k):
        dst = wbuf.at[slot, w_rows(part, k)]
        pltpu.make_async_copy(dst, dst, w_recv.at[slot - 1, part, k]).wait()

    def direct_early(k):
        return w_direct(0, 1, early_1, k), w_direct(1, 2, early_2, k)

    def direct_late(k):
        return w_direct(2, 1, 0, k), w_direct(3, 2, 1, k)

    def pass_early(k):
        to_1 = jnp.where(odd == 1, token, right)
        to_2 = jnp.where(odd == 1, token, left)
        return (
            w_pass(4, 1, early_1, k, 1 + 2 * odd, jnp.where(odd == 1, up, image), to_1),
            w_pass(5, 2, early_2, k, 2 + odd, jnp.where(odd == 1, down, image), to_2),
        )

    def pass_late(k):
        return w_pass(2, 3, 0, k, 3, image, right), w_pass(3, 3, 1, k, 3, image, left)

    for k in range(PARTS):
        for copy in direct_early(k):
            copy.start()

    @pl.when(odd == 0)
    def _():
        for k in range(PARTS):
            for copy in direct_late(k):
                copy.start()

    hid_out = pltpu.make_async_remote_copy(
        src_ref=hidden_ref.at[:, 0],
        dst_ref=hid.at[:, core],
        send_sem=hid_sem.at[0],
        recv_sem=hid_sem.at[1],
        device_id=(image, partner),
        device_id_type=MESH,
    )
    hid_out.start()

    def kv_pairs(head, branch):
        lanes = pl.ds(pl.multiple_of(head * HD, HD), HD)
        return (
            (key_ref.at[branch, 0, :, lanes], kbuf.at[token], 0),
            (value_ref.at[branch, 0, :, lanes], vbuf.at[token], 1),
        )

    def kv_start(head, branch, target):
        for src, dst, kind in kv_pairs(head, branch):
            pltpu.make_async_remote_copy(
                src_ref=src,
                dst_ref=dst,
                send_sem=kv_send.at[kind],
                recv_sem=kv_recv.at[kind],
                device_id=(image, target),
                device_id_type=MESH,
            ).start()

    for down_rows, right_cols in OFFSETS:
        to_row, to_col = (row + down_rows) & (SIDE - 1), (col + right_cols) & (SIDE - 1)
        to_head, there = head_of(to_row, to_col)
        to_chip = to_row * SIDE + to_col

        @pl.when(there)
        def _():
            for branch in range(2):
                kv_start(to_head, branch, to_chip * 2 + branch)

    @pl.when(has_head)
    def _():
        kv_start(my_head, 1 - core, partner)
        for src, dst, kind in kv_pairs(my_head, core):
            pltpu.make_async_copy(src, dst, kv_recv.at[kind]).start()

    @pl.loop(0, token_count)
    def _(tile):
        slot = jnp.int32(0)
        for j in range(slots):
            hit = (tiles_ref[0, j] == tile) & (count_ref[0] > j)
            slot = jnp.where(hit, jnp.int32(j), slot)
        slot_of[tile] = slot

    rows_all = 4 * TILE
    width = 256

    def project(slot, owner, start, size, is_first):
        features = pl.ds(pl.multiple_of(owner * depth + start, 128), size)
        w_part = pl.ds(pl.multiple_of(start, 128), size)

        @pl.loop(0, half_cols // width)
        def _(step):
            cols = pl.ds(pl.multiple_of(step * width, width), width)
            part = jnp.dot(
                hid[:, :, :, features].reshape(rows_all, size),
                wbuf[slot, w_part, cols],
                preferred_element_type=jnp.float32,
            ).reshape(2, 2, TILE, width)
            if is_first:
                acc[:, :, :, cols] = part
            else:
                acc[:, :, :, cols] += part

    w_own.wait()
    hid_own.wait()
    hid_out.wait_recv()
    project(0, image, 0, depth, True)
    for k in range(PARTS):
        first, second = pass_early(k)
        w_wait(1, early_1, k)
        first.start()
        w_wait(2, early_2, k)
        second.start()
    project(1, down, early_1 * half, half, False)
    project(2, up, early_2 * half, half, False)

    @pl.when(odd == 1)
    def _():
        for k in range(PARTS):
            first, second = pass_late(k)
            w_wait(3, 0, k)
            first.start()
            w_wait(3, 1, k)
            second.start()

    for k in range(PARTS):
        w_wait(1, 1 - early_1, k)
    project(1, down, (1 - early_1) * half, half, False)
    for k in range(PARTS):
        w_wait(2, 1 - early_2, k)
    project(2, up, (1 - early_2) * half, half, False)

    @pl.when(odd == 0)
    def _():
        for k in range(PARTS):
            w_wait(3, 0, k)
            w_wait(3, 1, k)

    project(3, far, 0, depth, False)

    rows = TILE // STAGES

    def q_start(stage, head, branch, target):
        pltpu.make_async_remote_copy(
            src_ref=qsend.at[stage, branch, head - core * half_heads],
            dst_ref=qbuf.at[stage, pl.ds(chip * 2, 2)],
            send_sem=q_send,
            recv_sem=q_recv.at[stage],
            device_id=(image, target),
            device_id_type=MESH,
        ).start()

    owns_head = has_head & (row >> 1 == core)
    for stage in range(STAGES):
        for head in range(half_heads):
            block = acc[:, :, stage * rows : (stage + 1) * rows, head * HD : (head + 1) * HD]
            qsend[stage, :, head] = block.astype(jnp.bfloat16)

        for step in range(2 * SIDE):
            to_row = 2 * core + ((row + step) & 1)
            to_col = (col + step + step // SIDE) & (SIDE - 1)
            to_head, there = head_of(to_row, to_col)
            to_chip = to_row * SIDE + to_col

            @pl.when(there & (to_chip != chip))
            def _():
                for branch in range(2):
                    q_start(stage, to_head, branch, to_chip * 2 + branch)

        @pl.when(owns_head)
        def _():
            q_start(stage, my_head, 1 - core, partner)
            pltpu.make_async_copy(
                qsend.at[stage, core, my_head - core * half_heads],
                qbuf.at[stage, pl.ds(chip * 2, 2)],
                q_recv.at[stage],
            ).start()

    share = rows // 2
    mine_rows = pl.ds(pl.multiple_of(core * share, share), share)
    sent_rows = pl.ds(pl.multiple_of((1 - core) * share, share), share)
    factor = LOG2E / math.sqrt(HD)
    span = 8
    chunk = span * TILE
    chunks = token_count // span
    height = slots * rows

    def exchange(stage):
        return pltpu.make_async_remote_copy(
            src_ref=attended.at[stage, :, sent_rows],
            dst_ref=other.at[stage],
            send_sem=x_send.at[stage],
            recv_sem=x_recv.at[stage],
            device_id=(image, partner),
            device_id_type=MESH,
        )

    def o_refs(stage, target):
        lanes = pl.ds(pl.multiple_of(my_head * HD, HD), HD)
        put = pl.ds(pl.multiple_of(stage * rows + core * share, share), share)
        return osend.at[stage, target], arrived.at[put, lanes]

    def o_start(stage, target):
        src, dst = o_refs(stage, target)
        pltpu.make_async_remote_copy(
            src_ref=src,
            dst_ref=dst,
            send_sem=o_send,
            recv_sem=o_recv,
            device_id=(image, target),
            device_id_type=MESH,
        ).start()

    def attention(stage):
        qnow[...] = qbuf[stage]
        query = jnp.concatenate([qnow[tiles_ref[0, j]] for j in range(slots)], axis=0)
        peak = jnp.full((height, 128), -jnp.inf, jnp.float32)
        for part in range(chunks):
            keys = kbuf[part * span : (part + 1) * span].reshape(chunk, HD)
            logits = lax.dot_general(
                query, keys, (((1,), (1,)), ((), ())), preferred_element_type=jnp.float32
            )
            score[:, part * chunk : (part + 1) * chunk] = logits
            for lane in range(span):
                peak = jnp.maximum(peak, logits[:, lane * 128 : (lane + 1) * 128])
        top = jnp.max(peak, axis=-1, keepdims=True) * factor
        total = jnp.zeros((height, 128), jnp.float32)
        summed = jnp.zeros((height, HD), jnp.float32)
        for part in range(chunks):
            values = vbuf[part * span : (part + 1) * span].reshape(chunk, HD)
            weight = jnp.exp2(score[:, part * chunk : (part + 1) * chunk] * factor - top)
            for lane in range(span):
                total = total + weight[:, lane * 128 : (lane + 1) * 128]
            summed = summed + jnp.dot(
                weight.astype(jnp.bfloat16), values, preferred_element_type=jnp.float32
            )
        summed = summed / jnp.sum(total, axis=-1, keepdims=True)
        attended[stage] = summed.reshape(slots, rows, HD)

    def deliver(stage):
        exchange(stage).wait_recv()
        scale = guide_ref[0]
        mine = attended[stage, :, mine_rows]
        theirs = other[stage]
        cond = jnp.where(core == 0, mine, theirs)
        uncond = jnp.where(core == 0, theirs, mine)
        guided[stage] = (uncond + scale * (cond - uncond)).astype(jnp.bfloat16)

        for tile in range(token_count):
            osend[stage, tile] = guided[stage, slot_of[tile]]

        for down_rows, right_cols in OFFSETS:
            to_row, to_col = (row + down_rows) & (SIDE - 1), (col + right_cols) & (SIDE - 1)
            for to_core in range(2):
                o_start(stage, (to_row * SIDE + to_col) * 2 + to_core)
        o_start(stage, partner)
        src, dst = o_refs(stage, token)
        pltpu.make_async_copy(src, dst, o_recv).start()

    @pl.when(has_head)
    def _():
        pltpu.make_async_copy(kbuf, kbuf, kv_recv.at[0]).wait()
        pltpu.make_async_copy(vbuf, vbuf, kv_recv.at[1]).wait()

        @pl.loop(0, STAGES + 1)
        def _(stage):
            @pl.when(stage < STAGES)
            def _():
                pltpu.make_async_copy(qbuf.at[stage], qbuf.at[stage], q_recv.at[stage]).wait()
                attention(stage)
                exchange(stage).start()

            @pl.when(stage > 0)
            def _():
                deliver(stage - 1)

    hid_out.wait_send()
    for k in range(PARTS):
        for copy in direct_early(k) + pass_early(k):
            copy.wait_send()

    @pl.when(odd == 0)
    def _():
        for k in range(PARTS):
            for copy in direct_late(k):
                copy.wait_send()

    @pl.when(odd == 1)
    def _():
        for k in range(PARTS):
            for copy in pass_late(k):
                copy.wait_send()

    def sent(ref, sem):
        pltpu.make_async_copy(ref, ref, sem).wait()

    @pl.when(has_head)
    def _():
        sent(kbuf.at[pl.ds(0, 2 * heads - 1)], kv_send.at[0])
        sent(vbuf.at[pl.ds(0, 2 * heads - 1)], kv_send.at[1])
        sent(osend.at[:, pl.ds(0, token_count - 1)], o_send)
        for stage in range(STAGES):
            exchange(stage).wait_send()

    @pl.when(jnp.logical_not(has_head))
    def _():
        sent(kbuf.at[pl.ds(0, 2 * heads)], kv_send.at[0])
        sent(vbuf.at[pl.ds(0, 2 * heads)], kv_send.at[1])

    @pl.when(owns_head)
    def _():
        sent(qbuf.at[:, pl.ds(0, 4 * half_heads - 2)], q_send)

    @pl.when(jnp.logical_not(owns_head))
    def _():
        sent(qbuf.at[:, pl.ds(0, 4 * half_heads)], q_send)

    pasted = jnp.int32(0)
    for j in range(slots):
        hit = (tiles_ref[0, j] == token) & (count_ref[0] > j)
        pasted = jnp.where(hit, jnp.int32(1), pasted)
    cached_own.wait()
    pltpu.make_async_copy(arrived, arrived, o_recv).wait()
    out_ref[0] = jnp.where(pasted == 1, arrived[...], cached[...])


def body(hidden, key_cache, value_cache, cached_out, w_query, guide, masked_tiles, mask_count):
    tokens = 2 * SIDE * SIDE
    inner = key_cache.shape[3]
    heads = inner // HD
    slots = masked_tiles.shape[1]
    width = hidden.shape[3]
    images = width // w_query.shape[0]
    rows = TILE // STAGES
    dma = pltpu.SemaphoreType.DMA
    return pl.pallas_call(
        kernel,
        out_shape=jax.ShapeDtypeStruct((1, TILE, inner), jnp.bfloat16),
        in_specs=[pl.BlockSpec(memory_space=pltpu.SMEM)] * 3
        + [pl.BlockSpec(memory_space=pl.ANY)] * 5,
        out_specs=pl.BlockSpec(memory_space=pltpu.VMEM),
        scratch_shapes=[
            pltpu.VMEM((2, 2, TILE, width), jnp.bfloat16),
            pltpu.VMEM((images, w_query.shape[0], inner // 2), jnp.bfloat16),
            pltpu.VMEM((2, 2, TILE, inner // 2), jnp.float32),
            pltpu.VMEM((STAGES, 2, heads // 2, 2, rows, HD), jnp.bfloat16),
            pltpu.VMEM((STAGES, tokens, rows, HD), jnp.bfloat16),
            pltpu.VMEM((tokens, rows, HD), jnp.bfloat16),
            pltpu.VMEM((tokens, TILE, HD), jnp.bfloat16),
            pltpu.VMEM((tokens, TILE, HD), jnp.bfloat16),
            pltpu.VMEM((slots * rows, tokens * TILE), jnp.float32),
            pltpu.VMEM((STAGES, slots, rows, HD), jnp.float32),
            pltpu.VMEM((STAGES, slots, rows // 2, HD), jnp.float32),
            pltpu.VMEM((STAGES, slots, rows // 2, HD), jnp.bfloat16),
            pltpu.VMEM((STAGES, tokens, rows // 2, HD), jnp.bfloat16),
            pltpu.VMEM((TILE, inner), jnp.bfloat16),
            pltpu.VMEM((TILE, inner), jnp.bfloat16),
            pltpu.SMEM((tokens,), jnp.int32),
            dma((3,)),
            dma((2,)),
            dma((6, PARTS)),
            dma((images - 1, 2, PARTS)),
            dma((2,)),
            dma((2,)),
            dma,
            dma((STAGES,)),
            dma((STAGES,)),
            dma((STAGES,)),
            dma,
            dma,
        ],
        compiler_params=pltpu.CompilerParams(
            collective_id=0, has_side_effects=True, vmem_limit_bytes=60 * 1024 * 1024
        ),
    )(masked_tiles, mask_count, guide, hidden, key_cache, value_cache, w_query, cached_out)


def solution(mesh):
    return jax.shard_map(
        body,
        mesh=mesh,
        in_specs=(
            P(None, "image", "token", None),
            P(None, "image", "token", None),
            P(None, "image", "token", None),
            P("image", "token", None),
            P("image", None),
            P("image"),
            P("image", None),
            P("image"),
        ),
        out_specs=P("image", "token", None),
        check_vma=False,
    )
```

```python
import functools
import math

import jax
import jax.numpy as jnp
from jax import lax
from jax.experimental import pallas as pl
from jax.experimental.pallas import tpu as pltpu
from jax.sharding import PartitionSpec as P

HD = 128
TILE = 128
SIDE = 4
STAGES = 4
PARTS = 6
DEPTH = 2
MESH = pl.DeviceIdType.MESH
LOG2E = 1.4426950408889634


def head_of(row, col):
    turn = (col - row - 1) & (SIDE - 1)
    last = SIDE - 2
    return row * (SIDE - 1) + jnp.minimum(turn, last), turn <= last


OFFSETS = tuple(
    ((2 * (i // SIDE) + i) % SIDE, (3 * (i // SIDE) + i) % SIDE) for i in range(1, SIDE * SIDE)
)


def kernel(
    tiles_ref,
    count_ref,
    guide_ref,
    hidden_ref,
    key_ref,
    value_ref,
    w_ref,
    cached_ref,
    out_ref,
    hid,
    wbuf,
    acc,
    qsend,
    qbuf,
    qnow,
    kbuf,
    vbuf,
    score,
    attended,
    other,
    guided,
    osend,
    arrived,
    cached,
    slot_of,
    local_sem,
    hid_sem,
    w_send,
    w_recv,
    kv_send,
    kv_recv,
    q_send,
    q_recv,
    x_send,
    x_recv,
    o_send,
    o_recv,
):
    image = lax.axis_index("image")
    token = lax.axis_index("token")
    images = hidden_ref.shape[3] // w_ref.shape[0]
    core = token & 1
    chip = token >> 1
    partner = token ^ 1
    row = chip >> 2
    col = chip & (SIDE - 1)
    my_head, has_head = head_of(row, col)
    odd = (row + col) & 1
    right = (row * SIDE + ((col + 1) & (SIDE - 1))) * 2 + core
    left = (row * SIDE + ((col - 1) & (SIDE - 1))) * 2 + core
    below = (((row + 1) & (SIDE - 1)) * SIDE + col) * 2 + core
    above = (((row - 1) & (SIDE - 1)) * SIDE + col) * 2 + core
    token_count = 2 * SIDE * SIDE
    heads = key_ref.shape[3] // HD
    half_heads = heads // 2
    depth = w_ref.shape[0]
    half_cols = w_ref.shape[1] // 2
    slots = tiles_ref.shape[1]
    up = (image + 1) & (images - 1)
    down = (image - 1) & (images - 1)
    far = image ^ 2

    my_cols = pl.ds(pl.multiple_of(core * half_cols, 128), half_cols)
    w_own = pltpu.make_async_copy(w_ref.at[:, my_cols], wbuf.at[0], local_sem.at[0])
    w_own.start()
    hid_own = pltpu.make_async_copy(hidden_ref.at[:, 0], hid.at[:, core], local_sem.at[1])
    hid_own.start()
    cached_own = pltpu.make_async_copy(cached_ref.at[0], cached, local_sem.at[2])
    cached_own.start()

    barrier = pltpu.get_barrier_semaphore()

    for near in (up, down):
        pl.semaphore_signal(barrier, inc=1, device_id=(near, token), device_id_type=MESH)
    for step in range(1, token_count):
        peer = token ^ step
        pl.semaphore_signal(barrier, inc=1, device_id=(image, peer), device_id_type=MESH)
    pl.semaphore_wait(barrier, token_count - 1 + 2)

    half = depth // 2
    piece = half // PARTS
    early_1, early_2 = 1 - odd, odd

    def w_rows(part, k):
        return pl.ds(pl.multiple_of(part * half + k * piece, piece), piece)

    def w_copy(index, src, slot, part, k, to_image, to_token):
        return pltpu.make_async_remote_copy(
            src_ref=src,
            dst_ref=wbuf.at[slot, w_rows(part, k)],
            send_sem=w_send.at[index, k],
            recv_sem=w_recv.at[slot - 1, part, k],
            device_id=(to_image, to_token),
            device_id_type=MESH,
        )

    def w_direct(index, slot, part, k):
        near = up if slot == 1 else down
        return w_copy(index, w_ref.at[w_rows(part, k), my_cols], slot, part, k, near, token)

    def w_pass(index, slot, part, k, new_slot, to_image, to_token):
        src = wbuf.at[slot, w_rows(part, k)]
        return w_copy(index, src, new_slot, part, k, to_image, to_token)

    def w_wait(slot, part, k):
        dst = wbuf.at[slot, w_rows(part, k)]
        pltpu.make_async_copy(dst, dst, w_recv.at[slot - 1, part, k]).wait()

    def direct_early(k):
        return w_direct(0, 1, early_1, k), w_direct(1, 2, early_2, k)

    def direct_late(k):
        return w_direct(2, 1, 0, k), w_direct(3, 2, 1, k)

    def near_pair(k):
        return (right, left) if k % 2 == 0 else (below, above)

    def pass_early(k):
        near_1, near_2 = near_pair(k)
        to_1 = jnp.where(odd == 1, token, near_1)
        to_2 = jnp.where(odd == 1, token, near_2)
        return (
            w_pass(4, 1, early_1, k, 1 + 2 * odd, jnp.where(odd == 1, up, image), to_1),
            w_pass(5, 2, early_2, k, 2 + odd, jnp.where(odd == 1, down, image), to_2),
        )

    def pass_late(k):
        near_1, near_2 = near_pair(k)
        return w_pass(2, 3, 0, k, 3, image, near_1), w_pass(3, 3, 1, k, 3, image, near_2)

    for k in range(PARTS):
        for copy in direct_early(k):
            copy.start()

    @pl.when(odd == 0)
    def _():
        for k in range(PARTS):
            for copy in direct_late(k):
                copy.start()

    hid_out = pltpu.make_async_remote_copy(
        src_ref=hidden_ref.at[:, 0],
        dst_ref=hid.at[:, core],
        send_sem=hid_sem.at[0],
        recv_sem=hid_sem.at[1],
        device_id=(image, partner),
        device_id_type=MESH,
    )
    hid_out.start()

    def kv_pairs(head, branch):
        lanes = pl.ds(pl.multiple_of(head * HD, HD), HD)
        return (
            (key_ref.at[branch, 0, :, lanes], kbuf.at[token], 0),
            (value_ref.at[branch, 0, :, lanes], vbuf.at[token], 1),
        )

    def kv_start(head, branch, target):
        for src, dst, kind in kv_pairs(head, branch):
            pltpu.make_async_remote_copy(
                src_ref=src,
                dst_ref=dst,
                send_sem=kv_send.at[kind],
                recv_sem=kv_recv.at[kind],
                device_id=(image, target),
                device_id_type=MESH,
            ).start()

    for down_rows, right_cols in OFFSETS:
        to_row, to_col = (row + down_rows) & (SIDE - 1), (col + right_cols) & (SIDE - 1)
        to_head, there = head_of(to_row, to_col)
        to_chip = to_row * SIDE + to_col

        @pl.when(there)
        def _():
            for branch in range(2):
                kv_start(to_head, branch, to_chip * 2 + branch)

    @pl.when(has_head)
    def _():
        kv_start(my_head, 1 - core, partner)
        for src, dst, kind in kv_pairs(my_head, core):
            pltpu.make_async_copy(src, dst, kv_recv.at[kind]).start()

    @pl.loop(0, token_count)
    def _(tile):
        slot = jnp.int32(0)
        for j in range(slots):
            hit = (tiles_ref[0, j] == tile) & (count_ref[0] > j)
            slot = jnp.where(hit, jnp.int32(j), slot)
        slot_of[tile] = slot

    rows_all = 4 * TILE
    width = 256

    def project(slot, owner, start, size, is_first):
        features = pl.ds(pl.multiple_of(owner * depth + start, 128), size)
        w_part = pl.ds(pl.multiple_of(start, 128), size)

        @pl.loop(0, half_cols // width)
        def _(step):
            cols = pl.ds(pl.multiple_of(step * width, width), width)
            part = jnp.dot(
                hid[:, :, :, features].reshape(rows_all, size),
                wbuf[slot, w_part, cols],
                preferred_element_type=jnp.float32,
            ).reshape(2, 2, TILE, width)
            if is_first:
                acc[:, :, :, cols] = part
            else:
                acc[:, :, :, cols] += part

    w_own.wait()
    hid_own.wait()
    hid_out.wait_recv()
    project(0, image, 0, depth, True)
    for k in range(PARTS):
        first, second = pass_early(k)
        w_wait(1, early_1, k)
        first.start()
        w_wait(2, early_2, k)
        second.start()
    project(1, down, early_1 * half, half, False)
    project(2, up, early_2 * half, half, False)

    @pl.when(odd == 1)
    def _():
        for k in range(PARTS):
            first, second = pass_late(k)
            w_wait(3, 0, k)
            first.start()
            w_wait(3, 1, k)
            second.start()

    for k in range(PARTS):
        w_wait(1, 1 - early_1, k)
    project(1, down, (1 - early_1) * half, half, False)
    for k in range(PARTS):
        w_wait(2, 1 - early_2, k)
    project(2, up, (1 - early_2) * half, half, False)

    @pl.when(odd == 0)
    def _():
        for k in range(PARTS):
            w_wait(3, 0, k)
            w_wait(3, 1, k)

    project(3, far, 0, depth, False)

    rows = TILE // STAGES

    def q_start(stage, head, branch, target):
        pltpu.make_async_remote_copy(
            src_ref=qsend.at[stage, branch, head - core * half_heads],
            dst_ref=qbuf.at[stage, pl.ds(chip * 2, 2)],
            send_sem=q_send.at[stage],
            recv_sem=q_recv.at[stage],
            device_id=(image, target),
            device_id_type=MESH,
        ).start()

    def sent(ref, sem):
        pltpu.make_async_copy(ref, ref, sem).wait()

    owns_head = has_head & (row >> 1 == core)

    def q_sent(stage):
        @pl.when(owns_head)
        def _():
            sent(qbuf.at[stage, pl.ds(0, 4 * half_heads - 2)], q_send.at[stage])

        @pl.when(jnp.logical_not(owns_head))
        def _():
            sent(qbuf.at[stage, pl.ds(0, 4 * half_heads)], q_send.at[stage])

    for stage in range(STAGES):
        for head in range(half_heads):
            block = acc[:, :, stage * rows : (stage + 1) * rows, head * HD : (head + 1) * HD]
            qsend[stage, :, head] = block.astype(jnp.bfloat16)
        if stage >= DEPTH:
            q_sent(stage - DEPTH)

        for step in range(2 * SIDE):
            to_row = 2 * core + ((row + step) & 1)
            to_col = (col + step + step // SIDE) & (SIDE - 1)
            to_head, there = head_of(to_row, to_col)
            to_chip = to_row * SIDE + to_col

            @pl.when(there & (to_chip != chip))
            def _():
                for branch in range(2):
                    q_start(stage, to_head, branch, to_chip * 2 + branch)

        @pl.when(owns_head)
        def _():
            q_start(stage, my_head, 1 - core, partner)
            pltpu.make_async_copy(
                qsend.at[stage, core, my_head - core * half_heads],
                qbuf.at[stage, pl.ds(chip * 2, 2)],
                q_recv.at[stage],
            ).start()

    share = rows // 2
    mine_rows = pl.ds(pl.multiple_of(core * share, share), share)
    sent_rows = pl.ds(pl.multiple_of((1 - core) * share, share), share)
    factor = LOG2E / math.sqrt(HD)
    span = 8
    chunk = span * TILE
    chunks = token_count // span
    height = slots * rows

    def exchange(stage):
        return pltpu.make_async_remote_copy(
            src_ref=attended.at[stage, :, sent_rows],
            dst_ref=other.at[stage],
            send_sem=x_send.at[stage],
            recv_sem=x_recv.at[stage],
            device_id=(image, partner),
            device_id_type=MESH,
        )

    def o_refs(stage, target):
        lanes = pl.ds(pl.multiple_of(my_head * HD, HD), HD)
        put = pl.ds(pl.multiple_of(stage * rows + core * share, share), share)
        return osend.at[stage, target], arrived.at[put, lanes]

    def o_start(stage, target):
        src, dst = o_refs(stage, target)
        pltpu.make_async_remote_copy(
            src_ref=src,
            dst_ref=dst,
            send_sem=o_send,
            recv_sem=o_recv,
            device_id=(image, target),
            device_id_type=MESH,
        ).start()

    def attention(stage):
        qnow[...] = qbuf[stage]
        query = jnp.concatenate([qnow[tiles_ref[0, j]] for j in range(slots)], axis=0)
        peak = jnp.full((height, 128), -jnp.inf, jnp.float32)
        for part in range(chunks):
            keys = kbuf[part * span : (part + 1) * span].reshape(chunk, HD)
            logits = lax.dot_general(
                query, keys, (((1,), (1,)), ((), ())), preferred_element_type=jnp.float32
            )
            score[:, part * chunk : (part + 1) * chunk] = logits
            for lane in range(span):
                peak = jnp.maximum(peak, logits[:, lane * 128 : (lane + 1) * 128])
        top = jnp.max(peak, axis=-1, keepdims=True) * factor
        total = jnp.zeros((height, 128), jnp.float32)
        summed = jnp.zeros((height, HD), jnp.float32)
        for part in range(chunks):
            values = vbuf[part * span : (part + 1) * span].reshape(chunk, HD)
            weight = jnp.exp2(score[:, part * chunk : (part + 1) * chunk] * factor - top)
            for lane in range(span):
                total = total + weight[:, lane * 128 : (lane + 1) * 128]
            summed = summed + jnp.dot(
                weight.astype(jnp.bfloat16), values, preferred_element_type=jnp.float32
            )
        summed = summed / jnp.sum(total, axis=-1, keepdims=True)
        attended[stage] = summed.reshape(slots, rows, HD)

    def deliver(stage):
        exchange(stage).wait_recv()
        scale = guide_ref[0]
        mine = attended[stage, :, mine_rows]
        theirs = other[stage]
        cond = jnp.where(core == 0, mine, theirs)
        uncond = jnp.where(core == 0, theirs, mine)
        guided[stage] = (uncond + scale * (cond - uncond)).astype(jnp.bfloat16)

        for tile in range(token_count):
            osend[stage, tile] = guided[stage, slot_of[tile]]

        for down_rows, right_cols in OFFSETS:
            to_row, to_col = (row + down_rows) & (SIDE - 1), (col + right_cols) & (SIDE - 1)
            for to_core in range(2):
                o_start(stage, (to_row * SIDE + to_col) * 2 + to_core)
        o_start(stage, partner)
        src, dst = o_refs(stage, token)
        pltpu.make_async_copy(src, dst, o_recv).start()

    @pl.when(has_head)
    def _():
        pltpu.make_async_copy(kbuf, kbuf, kv_recv.at[0]).wait()
        pltpu.make_async_copy(vbuf, vbuf, kv_recv.at[1]).wait()

        @pl.loop(0, STAGES + 1)
        def _(stage):
            @pl.when(stage < STAGES)
            def _():
                pltpu.make_async_copy(qbuf.at[stage], qbuf.at[stage], q_recv.at[stage]).wait()
                attention(stage)
                exchange(stage).start()

            @pl.when(stage > 0)
            def _():
                deliver(stage - 1)

    hid_out.wait_send()
    for k in range(PARTS):
        for copy in direct_early(k) + pass_early(k):
            copy.wait_send()

    @pl.when(odd == 0)
    def _():
        for k in range(PARTS):
            for copy in direct_late(k):
                copy.wait_send()

    @pl.when(odd == 1)
    def _():
        for k in range(PARTS):
            for copy in pass_late(k):
                copy.wait_send()

    @pl.when(has_head)
    def _():
        sent(kbuf.at[pl.ds(0, 2 * heads - 1)], kv_send.at[0])
        sent(vbuf.at[pl.ds(0, 2 * heads - 1)], kv_send.at[1])
        sent(osend.at[:, pl.ds(0, token_count - 1)], o_send)
        for stage in range(STAGES):
            exchange(stage).wait_send()

    @pl.when(jnp.logical_not(has_head))
    def _():
        sent(kbuf.at[pl.ds(0, 2 * heads)], kv_send.at[0])
        sent(vbuf.at[pl.ds(0, 2 * heads)], kv_send.at[1])

    for stage in range(STAGES - DEPTH, STAGES):
        q_sent(stage)

    pasted = jnp.int32(0)
    for j in range(slots):
        hit = (tiles_ref[0, j] == token) & (count_ref[0] > j)
        pasted = jnp.where(hit, jnp.int32(1), pasted)
    cached_own.wait()
    pltpu.make_async_copy(arrived, arrived, o_recv).wait()
    out_ref[0] = jnp.where(pasted == 1, arrived[...], cached[...])


def body(hidden, key_cache, value_cache, cached_out, w_query, guide, masked_tiles, mask_count):
    tokens = 2 * SIDE * SIDE
    inner = key_cache.shape[3]
    heads = inner // HD
    slots = masked_tiles.shape[1]
    width = hidden.shape[3]
    images = width // w_query.shape[0]
    rows = TILE // STAGES
    dma = pltpu.SemaphoreType.DMA
    return pl.pallas_call(
        kernel,
        out_shape=pltpu.VMEM((1, TILE, inner), jnp.bfloat16),
        in_specs=[pl.BlockSpec(memory_space=pltpu.SMEM)] * 3
        + [pl.BlockSpec(memory_space=pl.ANY)] * 5,
        out_specs=pl.BlockSpec(memory_space=pltpu.VMEM),
        scratch_shapes=[
            pltpu.VMEM((2, 2, TILE, width), jnp.bfloat16),
            pltpu.VMEM((images, w_query.shape[0], inner // 2), jnp.bfloat16),
            pltpu.VMEM((2, 2, TILE, inner // 2), jnp.float32),
            pltpu.VMEM((STAGES, 2, heads // 2, 2, rows, HD), jnp.bfloat16),
            pltpu.VMEM((STAGES, tokens, rows, HD), jnp.bfloat16),
            pltpu.VMEM((tokens, rows, HD), jnp.bfloat16),
            pltpu.VMEM((tokens, TILE, HD), jnp.bfloat16),
            pltpu.VMEM((tokens, TILE, HD), jnp.bfloat16),
            pltpu.VMEM((slots * rows, tokens * TILE), jnp.float32),
            pltpu.VMEM((STAGES, slots, rows, HD), jnp.float32),
            pltpu.VMEM((STAGES, slots, rows // 2, HD), jnp.float32),
            pltpu.VMEM((STAGES, slots, rows // 2, HD), jnp.bfloat16),
            pltpu.VMEM((STAGES, tokens, rows // 2, HD), jnp.bfloat16),
            pltpu.VMEM((TILE, inner), jnp.bfloat16),
            pltpu.VMEM((TILE, inner), jnp.bfloat16),
            pltpu.SMEM((tokens,), jnp.int32),
            dma((3,)),
            dma((2,)),
            dma((6, PARTS)),
            dma((images - 1, 2, PARTS)),
            dma((2,)),
            dma((2,)),
            dma((STAGES,)),
            dma((STAGES,)),
            dma((STAGES,)),
            dma((STAGES,)),
            dma,
            dma,
        ],
        compiler_params=pltpu.CompilerParams(
            collective_id=0, has_side_effects=True, vmem_limit_bytes=60 * 1024 * 1024
        ),
    )(masked_tiles, mask_count, guide, hidden, key_cache, value_cache, w_query, cached_out)


def solution(mesh):
    return jax.shard_map(
        body,
        mesh=mesh,
        in_specs=(
            P(None, "image", "token", None),
            P(None, "image", "token", None),
            P(None, "image", "token", None),
            P("image", "token", None),
            P("image", None),
            P("image"),
            P("image", None),
            P("image"),
        ),
        out_specs=P("image", "token", None),
        check_vma=False,
    )
```

```python
import functools
import math

import jax
import jax.numpy as jnp
from jax import lax
from jax.experimental import pallas as pl
from jax.experimental.pallas import tpu as pltpu
from jax.sharding import PartitionSpec as P

HD = 128
TILE = 128
SIDE = 4
STAGES = 4
PARTS = 12
DEPTH = 2
MESH = pl.DeviceIdType.MESH
LOG2E = 1.4426950408889634


def head_of(row, col):
    turn = (col - row - 1) & (SIDE - 1)
    last = SIDE - 2
    return row * (SIDE - 1) + jnp.minimum(turn, last), turn <= last


OFFSETS = tuple(
    ((2 * (i // SIDE) + i) % SIDE, (3 * (i // SIDE) + i) % SIDE) for i in range(1, SIDE * SIDE)
)


def kernel(
    tiles_ref,
    count_ref,
    guide_ref,
    hidden_ref,
    key_ref,
    value_ref,
    w_ref,
    cached_ref,
    out_ref,
    hid,
    wbuf,
    acc,
    qsend,
    qbuf,
    qnow,
    kbuf,
    vbuf,
    score,
    attended,
    other,
    guided,
    osend,
    arrived,
    cached,
    slot_of,
    local_sem,
    hid_sem,
    w_send,
    w_recv,
    kv_send,
    kv_recv,
    q_send,
    q_recv,
    x_send,
    x_recv,
    o_send,
    o_recv,
):
    image = lax.axis_index("image")
    token = lax.axis_index("token")
    images = hidden_ref.shape[3] // w_ref.shape[0]
    core = token & 1
    chip = token >> 1
    partner = token ^ 1
    row = chip >> 2
    col = chip & (SIDE - 1)
    my_head, has_head = head_of(row, col)
    odd = (row + col) & 1
    right = (row * SIDE + ((col + 1) & (SIDE - 1))) * 2 + core
    left = (row * SIDE + ((col - 1) & (SIDE - 1))) * 2 + core
    below = (((row + 1) & (SIDE - 1)) * SIDE + col) * 2 + core
    above = (((row - 1) & (SIDE - 1)) * SIDE + col) * 2 + core
    token_count = 2 * SIDE * SIDE
    heads = key_ref.shape[3] // HD
    half_heads = heads // 2
    depth = w_ref.shape[0]
    half_cols = w_ref.shape[1] // 2
    slots = tiles_ref.shape[1]
    up = (image + 1) & (images - 1)
    down = (image - 1) & (images - 1)
    far = image ^ 2

    my_cols = pl.ds(pl.multiple_of(core * half_cols, 128), half_cols)
    w_own = pltpu.make_async_copy(w_ref.at[:, my_cols], wbuf.at[0], local_sem.at[0])
    w_own.start()
    hid_own = pltpu.make_async_copy(hidden_ref.at[:, 0], hid.at[:, core], local_sem.at[1])
    hid_own.start()
    cached_own = pltpu.make_async_copy(cached_ref.at[0], cached, local_sem.at[2])
    cached_own.start()

    barrier = pltpu.get_barrier_semaphore()

    for near in (up, down):
        pl.semaphore_signal(barrier, inc=1, device_id=(near, token), device_id_type=MESH)
    for step in range(1, token_count):
        peer = token ^ step
        pl.semaphore_signal(barrier, inc=1, device_id=(image, peer), device_id_type=MESH)
    pl.semaphore_wait(barrier, token_count - 1 + 2)

    piece = depth // PARTS
    third = depth // 3
    even = odd == 0
    base = 4 * (1 - odd)

    def w_index(side, k):
        return k if side == 0 else PARTS - 1 - k

    def w_rows(side, k):
        return pl.ds(pl.multiple_of(w_index(side, k) * piece, piece), piece)

    def w_copy(kind, src, slot, side, k, to_image, to_token):
        return pltpu.make_async_remote_copy(
            src_ref=src,
            dst_ref=wbuf.at[slot, w_rows(side, k)],
            send_sem=w_send.at[kind],
            recv_sem=w_recv.at[slot - 1, w_index(side, k)],
            device_id=(to_image, to_token),
            device_id_type=MESH,
        )

    def w_direct(side, k):
        near = up if side == 0 else down
        w_copy(0, w_ref.at[w_rows(side, k), my_cols], 1 + side, side, k, near, token).start()

    def w_relay(side, k):
        near = up if side == 0 else down
        w_copy(0, wbuf.at[1 + side, w_rows(side, k)], 3, side, k, near, token).start()

    def w_pass(slot, side, k, turn):
        near = ((right, below), (left, above))[side][turn % 2]
        w_copy(1, wbuf.at[slot, w_rows(side, k)], slot, side, k, image, near).start()

    def w_wait(slot, side, k):
        dst = wbuf.at[slot, w_rows(side, k)]
        pltpu.make_async_copy(dst, dst, w_recv.at[slot - 1, w_index(side, k)]).wait()

    for k in range(4):
        for side in range(2):
            w_direct(side, base + k)

    hid_out = pltpu.make_async_remote_copy(
        src_ref=hidden_ref.at[:, 0],
        dst_ref=hid.at[:, core],
        send_sem=hid_sem.at[0],
        recv_sem=hid_sem.at[1],
        device_id=(image, partner),
        device_id_type=MESH,
    )
    hid_out.start()

    def kv_pairs(head, branch):
        lanes = pl.ds(pl.multiple_of(head * HD, HD), HD)
        return (
            (key_ref.at[branch, 0, :, lanes], kbuf.at[token], 0),
            (value_ref.at[branch, 0, :, lanes], vbuf.at[token], 1),
        )

    def kv_start(head, branch, target):
        for src, dst, kind in kv_pairs(head, branch):
            pltpu.make_async_remote_copy(
                src_ref=src,
                dst_ref=dst,
                send_sem=kv_send.at[kind],
                recv_sem=kv_recv.at[kind],
                device_id=(image, target),
                device_id_type=MESH,
            ).start()

    for down_rows, right_cols in OFFSETS:
        to_row, to_col = (row + down_rows) & (SIDE - 1), (col + right_cols) & (SIDE - 1)
        to_head, there = head_of(to_row, to_col)
        to_chip = to_row * SIDE + to_col

        @pl.when(there)
        def _():
            for branch in range(2):
                kv_start(to_head, branch, to_chip * 2 + branch)

    @pl.when(has_head)
    def _():
        kv_start(my_head, 1 - core, partner)
        for src, dst, kind in kv_pairs(my_head, core):
            pltpu.make_async_copy(src, dst, kv_recv.at[kind]).start()

    @pl.loop(0, token_count)
    def _(tile):
        slot = jnp.int32(0)
        for j in range(slots):
            hit = (tiles_ref[0, j] == tile) & (count_ref[0] > j)
            slot = jnp.where(hit, jnp.int32(j), slot)
        slot_of[tile] = slot

    rows_all = 4 * TILE
    width = 256

    def project(slot, start, size, is_first=False):
        owner = jnp.where(slot == 0, image, jnp.where(slot == 1, down, jnp.where(slot == 2, up, far)))
        features = pl.ds(pl.multiple_of(owner * depth + start, 128), size)
        w_part = pl.ds(pl.multiple_of(start, 128), size)

        @pl.loop(0, half_cols // width)
        def _(step):
            cols = pl.ds(pl.multiple_of(step * width, width), width)
            part = jnp.dot(
                hid[:, :, :, features].reshape(rows_all, size),
                wbuf[slot, w_part, cols],
                preferred_element_type=jnp.float32,
            ).reshape(2, 2, TILE, width)
            if is_first:
                acc[:, :, :, cols] = part
            else:
                acc[:, :, :, cols] += part

    w_own.wait()
    hid_own.wait()
    hid_out.wait_recv()
    project(0, 0, depth, True)
    for k in range(4):
        for side in range(2):
            w_wait(1 + side, side, base + k)
            if k < 2:
                w_relay(side, base + k)
            w_pass(1 + side, side, base + k, k)

        if k == 1:

            @pl.when(even)
            def _():
                for late in range(4):
                    for side in range(2):
                        w_direct(side, 8 + late)

        if k >= 2:

            @pl.when(odd == 1)
            def _():
                for side in range(2):
                    w_relay(side, k)

    near_0, near_1 = (1 - odd) * third, (1 + odd) * third
    project(1, near_0, third)
    project(2, near_1, third)

    @pl.when(even)
    def _():
        for k in range(4, 6):
            for side in range(2):
                w_wait(3, side, k)
                w_pass(3, side, k, k)
        for k in range(8, 12):
            for side in range(2):
                w_wait(1 + side, side, k)
                w_pass(1 + side, side, k, k)

    @pl.when(odd == 1)
    def _():
        for k in range(4):
            for side in range(2):
                w_wait(3, side, k)
                w_pass(3, side, k, k)

    project(1 + 2 * odd, 2 * third * (1 - odd), third)
    project(2 + odd, 2 * third * odd, third)

    for side in range(2):
        for k in range(4):
            w_wait(1 + side, side, 4 * odd + k)
    project(1, odd * third, third)
    project(2, (2 - odd) * third, third)

    @pl.when(odd == 1)
    def _():
        for side in range(2):
            for k in range(4, 6):
                w_wait(3, side, k)

    project(3, third, third)
    last_0, last_1 = 3 - 2 * odd, 3 - odd
    for side in range(2):
        for k in range(4):
            w_wait((last_0, last_1)[side], side, 8 * odd + k)
    project(last_0, 2 * third * odd, third)
    project(last_1, 2 * third * (1 - odd), third)

    rows = TILE // STAGES

    def q_start(stage, head, branch, target):
        pltpu.make_async_remote_copy(
            src_ref=qsend.at[stage, branch, head - core * half_heads],
            dst_ref=qbuf.at[stage, pl.ds(chip * 2, 2)],
            send_sem=q_send.at[stage],
            recv_sem=q_recv.at[stage],
            device_id=(image, target),
            device_id_type=MESH,
        ).start()

    def sent(ref, sem):
        pltpu.make_async_copy(ref, ref, sem).wait()

    owns_head = has_head & (row >> 1 == core)

    def q_sent(stage):
        @pl.when(owns_head)
        def _():
            sent(qbuf.at[stage, pl.ds(0, 4 * half_heads - 2)], q_send.at[stage])

        @pl.when(jnp.logical_not(owns_head))
        def _():
            sent(qbuf.at[stage, pl.ds(0, 4 * half_heads)], q_send.at[stage])

    for stage in range(STAGES):
        for head in range(half_heads):
            block = acc[:, :, stage * rows : (stage + 1) * rows, head * HD : (head + 1) * HD]
            qsend[stage, :, head] = block.astype(jnp.bfloat16)
        if stage >= DEPTH:
            q_sent(stage - DEPTH)

        for step in range(2 * SIDE):
            to_row = 2 * core + ((row + step) & 1)
            to_col = (col + step + step // SIDE) & (SIDE - 1)
            to_head, there = head_of(to_row, to_col)
            to_chip = to_row * SIDE + to_col

            @pl.when(there & (to_chip != chip))
            def _():
                for branch in range(2):
                    q_start(stage, to_head, branch, to_chip * 2 + branch)

        @pl.when(owns_head)
        def _():
            q_start(stage, my_head, 1 - core, partner)
            pltpu.make_async_copy(
                qsend.at[stage, core, my_head - core * half_heads],
                qbuf.at[stage, pl.ds(chip * 2, 2)],
                q_recv.at[stage],
            ).start()

    share = rows // 2
    mine_rows = pl.ds(pl.multiple_of(core * share, share), share)
    sent_rows = pl.ds(pl.multiple_of((1 - core) * share, share), share)
    factor = LOG2E / math.sqrt(HD)
    span = 8
    chunk = span * TILE
    chunks = token_count // span
    height = slots * rows

    def exchange(stage):
        return pltpu.make_async_remote_copy(
            src_ref=attended.at[stage, :, sent_rows],
            dst_ref=other.at[stage],
            send_sem=x_send.at[stage],
            recv_sem=x_recv.at[stage],
            device_id=(image, partner),
            device_id_type=MESH,
        )

    def o_refs(stage, target):
        lanes = pl.ds(pl.multiple_of(my_head * HD, HD), HD)
        put = pl.ds(pl.multiple_of(stage * rows + core * share, share), share)
        return osend.at[stage, target], arrived.at[put, lanes]

    def o_start(stage, target):
        src, dst = o_refs(stage, target)
        pltpu.make_async_remote_copy(
            src_ref=src,
            dst_ref=dst,
            send_sem=o_send,
            recv_sem=o_recv,
            device_id=(image, target),
            device_id_type=MESH,
        ).start()

    def attention(stage):
        qnow[...] = qbuf[stage]
        query = jnp.concatenate([qnow[tiles_ref[0, j]] for j in range(slots)], axis=0)
        peak = jnp.full((height, 128), -jnp.inf, jnp.float32)
        for part in range(chunks):
            keys = kbuf[part * span : (part + 1) * span].reshape(chunk, HD)
            logits = lax.dot_general(
                query, keys, (((1,), (1,)), ((), ())), preferred_element_type=jnp.float32
            )
            score[:, part * chunk : (part + 1) * chunk] = logits
            for lane in range(span):
                peak = jnp.maximum(peak, logits[:, lane * 128 : (lane + 1) * 128])
        top = jnp.max(peak, axis=-1, keepdims=True) * factor
        total = jnp.zeros((height, 128), jnp.float32)
        summed = jnp.zeros((height, HD), jnp.float32)
        for part in range(chunks):
            values = vbuf[part * span : (part + 1) * span].reshape(chunk, HD)
            weight = jnp.exp2(score[:, part * chunk : (part + 1) * chunk] * factor - top)
            for lane in range(span):
                total = total + weight[:, lane * 128 : (lane + 1) * 128]
            summed = summed + jnp.dot(
                weight.astype(jnp.bfloat16), values, preferred_element_type=jnp.float32
            )
        summed = summed / jnp.sum(total, axis=-1, keepdims=True)
        attended[stage] = summed.reshape(slots, rows, HD)

    def deliver(stage):
        exchange(stage).wait_recv()
        scale = guide_ref[0]
        mine = attended[stage, :, mine_rows]
        theirs = other[stage]
        cond = jnp.where(core == 0, mine, theirs)
        uncond = jnp.where(core == 0, theirs, mine)
        guided[stage] = (uncond + scale * (cond - uncond)).astype(jnp.bfloat16)

        for tile in range(token_count):
            osend[stage, tile] = guided[stage, slot_of[tile]]

        for down_rows, right_cols in OFFSETS:
            to_row, to_col = (row + down_rows) & (SIDE - 1), (col + right_cols) & (SIDE - 1)
            for to_core in range(2):
                o_start(stage, (to_row * SIDE + to_col) * 2 + to_core)
        o_start(stage, partner)
        src, dst = o_refs(stage, token)
        pltpu.make_async_copy(src, dst, o_recv).start()

    @pl.when(has_head)
    def _():
        pltpu.make_async_copy(kbuf, kbuf, kv_recv.at[0]).wait()
        pltpu.make_async_copy(vbuf, vbuf, kv_recv.at[1]).wait()

        @pl.loop(0, STAGES + 1)
        def _(stage):
            @pl.when(stage < STAGES)
            def _():
                pltpu.make_async_copy(qbuf.at[stage], qbuf.at[stage], q_recv.at[stage]).wait()
                attention(stage)
                exchange(stage).start()

            @pl.when(stage > 0)
            def _():
                deliver(stage - 1)

    hid_out.wait_send()

    @pl.when(even)
    def _():
        for kind in range(2):
            sent(wbuf.at[pl.ds(0, 2), pl.ds(0, 10 * piece)], w_send.at[kind])

    @pl.when(odd == 1)
    def _():
        for kind in range(2):
            sent(wbuf.at[pl.ds(0, 2), pl.ds(0, 8 * piece)], w_send.at[kind])

    @pl.when(has_head)
    def _():
        sent(kbuf.at[pl.ds(0, 2 * heads - 1)], kv_send.at[0])
        sent(vbuf.at[pl.ds(0, 2 * heads - 1)], kv_send.at[1])
        sent(osend.at[:, pl.ds(0, token_count - 1)], o_send)
        for stage in range(STAGES):
            exchange(stage).wait_send()

    @pl.when(jnp.logical_not(has_head))
    def _():
        sent(kbuf.at[pl.ds(0, 2 * heads)], kv_send.at[0])
        sent(vbuf.at[pl.ds(0, 2 * heads)], kv_send.at[1])

    for stage in range(STAGES - DEPTH, STAGES):
        q_sent(stage)

    pasted = jnp.int32(0)
    for j in range(slots):
        hit = (tiles_ref[0, j] == token) & (count_ref[0] > j)
        pasted = jnp.where(hit, jnp.int32(1), pasted)
    cached_own.wait()
    pltpu.make_async_copy(arrived, arrived, o_recv).wait()
    out_ref[0] = jnp.where(pasted == 1, arrived[...], cached[...])


def body(hidden, key_cache, value_cache, cached_out, w_query, guide, masked_tiles, mask_count):
    tokens = 2 * SIDE * SIDE
    inner = key_cache.shape[3]
    heads = inner // HD
    slots = masked_tiles.shape[1]
    width = hidden.shape[3]
    images = width // w_query.shape[0]
    rows = TILE // STAGES
    dma = pltpu.SemaphoreType.DMA
    return pl.pallas_call(
        kernel,
        out_shape=pltpu.VMEM((1, TILE, inner), jnp.bfloat16),
        in_specs=[pl.BlockSpec(memory_space=pltpu.SMEM)] * 3
        + [pl.BlockSpec(memory_space=pl.ANY)] * 5,
        out_specs=pl.BlockSpec(memory_space=pltpu.VMEM),
        scratch_shapes=[
            pltpu.VMEM((2, 2, TILE, width), jnp.bfloat16),
            pltpu.VMEM((images, w_query.shape[0], inner // 2), jnp.bfloat16),
            pltpu.VMEM((2, 2, TILE, inner // 2), jnp.float32),
            pltpu.VMEM((STAGES, 2, heads // 2, 2, rows, HD), jnp.bfloat16),
            pltpu.VMEM((STAGES, tokens, rows, HD), jnp.bfloat16),
            pltpu.VMEM((tokens, rows, HD), jnp.bfloat16),
            pltpu.VMEM((tokens, TILE, HD), jnp.bfloat16),
            pltpu.VMEM((tokens, TILE, HD), jnp.bfloat16),
            pltpu.VMEM((slots * rows, tokens * TILE), jnp.float32),
            pltpu.VMEM((STAGES, slots, rows, HD), jnp.float32),
            pltpu.VMEM((STAGES, slots, rows // 2, HD), jnp.float32),
            pltpu.VMEM((STAGES, slots, rows // 2, HD), jnp.bfloat16),
            pltpu.VMEM((STAGES, tokens, rows // 2, HD), jnp.bfloat16),
            pltpu.VMEM((TILE, inner), jnp.bfloat16),
            pltpu.VMEM((TILE, inner), jnp.bfloat16),
            pltpu.SMEM((tokens,), jnp.int32),
            dma((3,)),
            dma((2,)),
            dma((2,)),
            dma((images - 1, PARTS)),
            dma((2,)),
            dma((2,)),
            dma((STAGES,)),
            dma((STAGES,)),
            dma((STAGES,)),
            dma((STAGES,)),
            dma,
            dma,
        ],
        compiler_params=pltpu.CompilerParams(
            collective_id=0, has_side_effects=True, vmem_limit_bytes=60 * 1024 * 1024
        ),
    )(masked_tiles, mask_count, guide, hidden, key_cache, value_cache, w_query, cached_out)


def solution(mesh):
    return jax.shard_map(
        body,
        mesh=mesh,
        in_specs=(
            P(None, "image", "token", None),
            P(None, "image", "token", None),
            P(None, "image", "token", None),
            P("image", "token", None),
            P("image", None),
            P("image"),
            P("image", None),
            P("image"),
        ),
        out_specs=P("image", "token", None),
        check_vma=False,
    )
```

```python
import functools
import math

import jax
import jax.numpy as jnp
from jax import lax
from jax.experimental import pallas as pl
from jax.experimental.pallas import tpu as pltpu
from jax.sharding import PartitionSpec as P

HD = 128
TILE = 128
SIDE = 4
STAGES = 4
PARTS = 6
DEPTH = 2
BLOCK = 32
SPAN = 8
MESH = pl.DeviceIdType.MESH
LOG2E = 1.4426950408889634


def head_of(row, col):
    turn = (col - row - 1) & (SIDE - 1)
    last = SIDE - 2
    return row * (SIDE - 1) + jnp.minimum(turn, last), turn <= last


OFFSETS = tuple(
    ((2 * (i // SIDE) + i) % SIDE, (3 * (i // SIDE) + i) % SIDE) for i in range(1, SIDE * SIDE)
)


def kernel(
    tiles_ref,
    count_ref,
    guide_ref,
    hidden_ref,
    key_ref,
    value_ref,
    w_ref,
    cached_ref,
    out_ref,
    hid,
    wbuf,
    acc,
    qsend,
    qbuf,
    qnow,
    kbuf,
    vbuf,
    query,
    score,
    heavy,
    totals,
    sums,
    attended,
    other,
    guided,
    osend,
    arrived,
    cached,
    slot_of,
    local_sem,
    hid_sem,
    w_send,
    w_recv,
    kv_send,
    kv_recv,
    q_send,
    q_recv,
    x_send,
    x_recv,
    o_send,
    o_recv,
):
    image = lax.axis_index("image")
    token = lax.axis_index("token")
    images = hidden_ref.shape[3] // w_ref.shape[0]
    core = token & 1
    chip = token >> 1
    partner = token ^ 1
    row = chip >> 2
    col = chip & (SIDE - 1)
    my_head, has_head = head_of(row, col)
    odd = (row + col) & 1
    right = (row * SIDE + ((col + 1) & (SIDE - 1))) * 2 + core
    left = (row * SIDE + ((col - 1) & (SIDE - 1))) * 2 + core
    below = (((row + 1) & (SIDE - 1)) * SIDE + col) * 2 + core
    above = (((row - 1) & (SIDE - 1)) * SIDE + col) * 2 + core
    token_count = 2 * SIDE * SIDE
    heads = key_ref.shape[3] // HD
    half_heads = heads // 2
    depth = w_ref.shape[0]
    half_cols = w_ref.shape[1] // 2
    slots = tiles_ref.shape[1]
    up = (image + 1) & (images - 1)
    down = (image - 1) & (images - 1)
    far = image ^ 2

    my_cols = pl.ds(pl.multiple_of(core * half_cols, 128), half_cols)
    w_own = pltpu.make_async_copy(w_ref.at[:, my_cols], wbuf.at[0], local_sem.at[0])
    w_own.start()
    hid_own = pltpu.make_async_copy(hidden_ref.at[:, 0], hid.at[:, core], local_sem.at[1])
    hid_own.start()
    cached_own = pltpu.make_async_copy(cached_ref.at[0], cached, local_sem.at[2])
    cached_own.start()

    barrier = pltpu.get_barrier_semaphore()

    for near in (up, down):
        pl.semaphore_signal(barrier, inc=1, device_id=(near, token), device_id_type=MESH)
    for step in range(1, token_count):
        peer = token ^ step
        pl.semaphore_signal(barrier, inc=1, device_id=(image, peer), device_id_type=MESH)
    pl.semaphore_wait(barrier, token_count - 1 + 2)

    half = depth // 2
    piece = half // PARTS
    early_1, early_2 = 1 - odd, odd

    def w_rows(part, k):
        return pl.ds(pl.multiple_of(part * half + k * piece, piece), piece)

    def w_copy(index, src, slot, part, k, to_image, to_token):
        return pltpu.make_async_remote_copy(
            src_ref=src,
            dst_ref=wbuf.at[slot, w_rows(part, k)],
            send_sem=w_send.at[index, k],
            recv_sem=w_recv.at[slot - 1, part, k],
            device_id=(to_image, to_token),
            device_id_type=MESH,
        )

    def w_direct(index, slot, part, k):
        near = up if slot == 1 else down
        return w_copy(index, w_ref.at[w_rows(part, k), my_cols], slot, part, k, near, token)

    def w_pass(index, slot, part, k, new_slot, to_image, to_token):
        src = wbuf.at[slot, w_rows(part, k)]
        return w_copy(index, src, new_slot, part, k, to_image, to_token)

    def w_wait(slot, part, k):
        dst = wbuf.at[slot, w_rows(part, k)]
        pltpu.make_async_copy(dst, dst, w_recv.at[slot - 1, part, k]).wait()

    def direct_early(k):
        return w_direct(0, 1, early_1, k), w_direct(1, 2, early_2, k)

    def direct_late(k):
        return w_direct(2, 1, 0, k), w_direct(3, 2, 1, k)

    def near_pair(k):
        return (right, left) if k % 2 == 0 else (below, above)

    def pass_early(k):
        near_1, near_2 = near_pair(k)
        to_1 = jnp.where(odd == 1, token, near_1)
        to_2 = jnp.where(odd == 1, token, near_2)
        return (
            w_pass(4, 1, early_1, k, 1 + 2 * odd, jnp.where(odd == 1, up, image), to_1),
            w_pass(5, 2, early_2, k, 2 + odd, jnp.where(odd == 1, down, image), to_2),
        )

    def pass_late(k):
        near_1, near_2 = near_pair(k)
        return w_pass(2, 3, 0, k, 3, image, near_1), w_pass(3, 3, 1, k, 3, image, near_2)

    for k in range(PARTS):
        for copy in direct_early(k):
            copy.start()

    @pl.when(odd == 0)
    def _():
        for k in range(PARTS):
            for copy in direct_late(k):
                copy.start()

    hid_out = pltpu.make_async_remote_copy(
        src_ref=hidden_ref.at[:, 0],
        dst_ref=hid.at[:, core],
        send_sem=hid_sem.at[0],
        recv_sem=hid_sem.at[1],
        device_id=(image, partner),
        device_id_type=MESH,
    )
    hid_out.start()

    def kv_pairs(head, branch):
        lanes = pl.ds(pl.multiple_of(head * HD, HD), HD)
        return (
            (key_ref.at[branch, 0, :, lanes], kbuf.at[token], 0),
            (value_ref.at[branch, 0, :, lanes], vbuf.at[token], 1),
        )

    def kv_start(head, branch, target):
        for src, dst, kind in kv_pairs(head, branch):
            pltpu.make_async_remote_copy(
                src_ref=src,
                dst_ref=dst,
                send_sem=kv_send.at[kind],
                recv_sem=kv_recv.at[kind],
                device_id=(image, target),
                device_id_type=MESH,
            ).start()

    for down_rows, right_cols in OFFSETS:
        to_row, to_col = (row + down_rows) & (SIDE - 1), (col + right_cols) & (SIDE - 1)
        to_head, there = head_of(to_row, to_col)
        to_chip = to_row * SIDE + to_col

        @pl.when(there)
        def _():
            for branch in range(2):
                kv_start(to_head, branch, to_chip * 2 + branch)

    @pl.when(has_head)
    def _():
        kv_start(my_head, 1 - core, partner)
        for src, dst, kind in kv_pairs(my_head, core):
            pltpu.make_async_copy(src, dst, kv_recv.at[kind]).start()

    @pl.loop(0, token_count)
    def _(tile):
        slot = jnp.int32(0)
        for j in range(slots):
            hit = (tiles_ref[0, j] == tile) & (count_ref[0] > j)
            slot = jnp.where(hit, jnp.int32(j), slot)
        slot_of[tile] = slot

    rows_all = 4 * TILE
    width = 256

    def project(slot, owner, start, size, is_first):
        features = pl.ds(pl.multiple_of(owner * depth + start, 128), size)
        w_part = pl.ds(pl.multiple_of(start, 128), size)

        @pl.loop(0, half_cols // width)
        def _(step):
            cols = pl.ds(pl.multiple_of(step * width, width), width)
            part = jnp.dot(
                hid[:, :, :, features].reshape(rows_all, size),
                wbuf[slot, w_part, cols],
                preferred_element_type=jnp.float32,
            ).reshape(2, 2, TILE, width)
            if is_first:
                acc[:, :, :, cols] = part
            else:
                acc[:, :, :, cols] += part

    w_own.wait()
    hid_own.wait()
    hid_out.wait_recv()
    project(0, image, 0, depth, True)
    for k in range(PARTS):
        first, second = pass_early(k)
        w_wait(1, early_1, k)
        first.start()
        w_wait(2, early_2, k)
        second.start()
    project(1, down, early_1 * half, half, False)
    project(2, up, early_2 * half, half, False)

    @pl.when(odd == 1)
    def _():
        for k in range(PARTS):
            first, second = pass_late(k)
            w_wait(3, 0, k)
            first.start()
            w_wait(3, 1, k)
            second.start()

    for k in range(PARTS):
        w_wait(1, 1 - early_1, k)
    project(1, down, (1 - early_1) * half, half, False)
    for k in range(PARTS):
        w_wait(2, 1 - early_2, k)
    project(2, up, (1 - early_2) * half, half, False)

    @pl.when(odd == 0)
    def _():
        for k in range(PARTS):
            w_wait(3, 0, k)
            w_wait(3, 1, k)

    project(3, far, 0, depth, False)

    rows = TILE // STAGES

    def q_start(stage, head, branch, target):
        pltpu.make_async_remote_copy(
            src_ref=qsend.at[stage, branch, head - core * half_heads],
            dst_ref=qbuf.at[stage, pl.ds(chip * 2, 2)],
            send_sem=q_send.at[stage],
            recv_sem=q_recv.at[stage],
            device_id=(image, target),
            device_id_type=MESH,
        ).start()

    def sent(ref, sem):
        pltpu.make_async_copy(ref, ref, sem).wait()

    owns_head = has_head & (row >> 1 == core)

    def q_sent(stage):
        @pl.when(owns_head)
        def _():
            sent(qbuf.at[stage, pl.ds(0, 4 * half_heads - 2)], q_send.at[stage])

        @pl.when(jnp.logical_not(owns_head))
        def _():
            sent(qbuf.at[stage, pl.ds(0, 4 * half_heads)], q_send.at[stage])

    for stage in range(STAGES):
        for head in range(half_heads):
            block = acc[:, :, stage * rows : (stage + 1) * rows, head * HD : (head + 1) * HD]
            qsend[stage, :, head] = block.astype(jnp.bfloat16)
        if stage >= DEPTH:
            q_sent(stage - DEPTH)

        for step in range(2 * SIDE):
            to_row = 2 * core + ((row + step) & 1)
            to_col = (col + step + step // SIDE) & (SIDE - 1)
            to_head, there = head_of(to_row, to_col)
            to_chip = to_row * SIDE + to_col

            @pl.when(there & (to_chip != chip))
            def _():
                for branch in range(2):
                    q_start(stage, to_head, branch, to_chip * 2 + branch)

        @pl.when(owns_head)
        def _():
            q_start(stage, my_head, 1 - core, partner)
            pltpu.make_async_copy(
                qsend.at[stage, core, my_head - core * half_heads],
                qbuf.at[stage, pl.ds(chip * 2, 2)],
                q_recv.at[stage],
            ).start()

    share = rows // 2
    mine_rows = pl.ds(pl.multiple_of(core * share, share), share)
    sent_rows = pl.ds(pl.multiple_of((1 - core) * share, share), share)
    factor = LOG2E / math.sqrt(HD)
    span = SPAN
    chunk = span * TILE
    chunks = token_count // span
    height = slots * rows

    def exchange(stage):
        return pltpu.make_async_remote_copy(
            src_ref=attended.at[stage, :, sent_rows],
            dst_ref=other.at[stage],
            send_sem=x_send.at[stage],
            recv_sem=x_recv.at[stage],
            device_id=(image, partner),
            device_id_type=MESH,
        )

    def o_refs(stage, target):
        lanes = pl.ds(pl.multiple_of(my_head * HD, HD), HD)
        put = pl.ds(pl.multiple_of(stage * rows + core * share, share), share)
        return osend.at[stage, target], arrived.at[put, lanes]

    def o_start(stage, target):
        src, dst = o_refs(stage, target)
        pltpu.make_async_remote_copy(
            src_ref=src,
            dst_ref=dst,
            send_sem=o_send,
            recv_sem=o_recv,
            device_id=(image, target),
            device_id_type=MESH,
        ).start()

    def attention(stage):
        qnow[...] = qbuf[stage]
        for j in range(slots):
            query[j * rows : (j + 1) * rows] = qnow[tiles_ref[0, j]]

        def logits(part):
            keys = kbuf[part * span : (part + 1) * span].reshape(chunk, HD)
            score[part % 2] = lax.dot_general(
                query[...], keys, (((1,), (1,)), ((), ())), preferred_element_type=jnp.float32
            )

        blocks = range(0, height, BLOCK)
        top = [None for _ in blocks]
        logits(0)
        for part in range(chunks):
            if part + 1 < chunks:
                logits(part + 1)
            shrink = []
            for index, low in enumerate(blocks):
                some = pl.ds(low, BLOCK)
                peak = score[part % 2, some, 0:128]
                for lane in range(1, span):
                    peak = jnp.maximum(peak, score[part % 2, some, lane * 128 : (lane + 1) * 128])
                peak = jnp.max(peak, axis=-1, keepdims=True) * factor
                if part > 0:
                    peak = jnp.maximum(peak, top[index])
                    shrink.append(jnp.exp2(top[index] - peak))
                top[index] = peak
                total = None
                for lane in range(span):
                    lanes = slice(lane * 128, (lane + 1) * 128)
                    weight = jnp.exp2(score[part % 2, some, lanes] * factor - peak)
                    heavy[part % 2, some, lanes] = weight.astype(jnp.bfloat16)
                    total = weight if total is None else total + weight
                if part > 0:
                    total = total + totals[some] * shrink[index]
                totals[some] = total
            values = vbuf[part * span : (part + 1) * span].reshape(chunk, HD)
            summed = jnp.dot(heavy[part % 2], values, preferred_element_type=jnp.float32)
            for index, low in enumerate(blocks):
                some = pl.ds(low, BLOCK)
                block = summed[low : low + BLOCK]
                if part > 0:
                    block = block + sums[some] * shrink[index]
                sums[some] = block
        done = sums[...] / jnp.sum(totals[...], axis=-1, keepdims=True)
        attended[stage] = done.reshape(slots, rows, HD)

    def deliver(stage):
        exchange(stage).wait_recv()
        scale = guide_ref[0]
        mine = attended[stage, :, mine_rows]
        theirs = other[stage]
        cond = jnp.where(core == 0, mine, theirs)
        uncond = jnp.where(core == 0, theirs, mine)
        guided[stage] = (uncond + scale * (cond - uncond)).astype(jnp.bfloat16)

        for tile in range(token_count):
            osend[stage, tile] = guided[stage, slot_of[tile]]

        for down_rows, right_cols in OFFSETS:
            to_row, to_col = (row + down_rows) & (SIDE - 1), (col + right_cols) & (SIDE - 1)
            for to_core in range(2):
                o_start(stage, (to_row * SIDE + to_col) * 2 + to_core)
        o_start(stage, partner)
        src, dst = o_refs(stage, token)
        pltpu.make_async_copy(src, dst, o_recv).start()

    @pl.when(has_head)
    def _():
        pltpu.make_async_copy(kbuf, kbuf, kv_recv.at[0]).wait()
        pltpu.make_async_copy(vbuf, vbuf, kv_recv.at[1]).wait()

        @pl.loop(0, STAGES + 1)
        def _(stage):
            @pl.when(stage < STAGES)
            def _():
                pltpu.make_async_copy(qbuf.at[stage], qbuf.at[stage], q_recv.at[stage]).wait()
                attention(stage)
                exchange(stage).start()

            @pl.when(stage > 0)
            def _():
                deliver(stage - 1)

    hid_out.wait_send()
    for k in range(PARTS):
        for copy in direct_early(k) + pass_early(k):
            copy.wait_send()

    @pl.when(odd == 0)
    def _():
        for k in range(PARTS):
            for copy in direct_late(k):
                copy.wait_send()

    @pl.when(odd == 1)
    def _():
        for k in range(PARTS):
            for copy in pass_late(k):
                copy.wait_send()

    @pl.when(has_head)
    def _():
        sent(kbuf.at[pl.ds(0, 2 * heads - 1)], kv_send.at[0])
        sent(vbuf.at[pl.ds(0, 2 * heads - 1)], kv_send.at[1])
        sent(osend.at[:, pl.ds(0, token_count - 1)], o_send)
        for stage in range(STAGES):
            exchange(stage).wait_send()

    @pl.when(jnp.logical_not(has_head))
    def _():
        sent(kbuf.at[pl.ds(0, 2 * heads)], kv_send.at[0])
        sent(vbuf.at[pl.ds(0, 2 * heads)], kv_send.at[1])

    for stage in range(STAGES - DEPTH, STAGES):
        q_sent(stage)

    pasted = jnp.int32(0)
    for j in range(slots):
        hit = (tiles_ref[0, j] == token) & (count_ref[0] > j)
        pasted = jnp.where(hit, jnp.int32(1), pasted)
    cached_own.wait()
    pltpu.make_async_copy(arrived, arrived, o_recv).wait()
    out_ref[0] = jnp.where(pasted == 1, arrived[...], cached[...])


def body(hidden, key_cache, value_cache, cached_out, w_query, guide, masked_tiles, mask_count):
    tokens = 2 * SIDE * SIDE
    inner = key_cache.shape[3]
    heads = inner // HD
    slots = masked_tiles.shape[1]
    width = hidden.shape[3]
    images = width // w_query.shape[0]
    rows = TILE // STAGES
    dma = pltpu.SemaphoreType.DMA
    return pl.pallas_call(
        kernel,
        out_shape=pltpu.VMEM((1, TILE, inner), jnp.bfloat16),
        in_specs=[pl.BlockSpec(memory_space=pltpu.SMEM)] * 3
        + [pl.BlockSpec(memory_space=pl.ANY)] * 5,
        out_specs=pl.BlockSpec(memory_space=pltpu.VMEM),
        scratch_shapes=[
            pltpu.VMEM((2, 2, TILE, width), jnp.bfloat16),
            pltpu.VMEM((images, w_query.shape[0], inner // 2), jnp.bfloat16),
            pltpu.VMEM((2, 2, TILE, inner // 2), jnp.float32),
            pltpu.VMEM((STAGES, 2, heads // 2, 2, rows, HD), jnp.bfloat16),
            pltpu.VMEM((STAGES, tokens, rows, HD), jnp.bfloat16),
            pltpu.VMEM((tokens, rows, HD), jnp.bfloat16),
            pltpu.VMEM((tokens, TILE, HD), jnp.bfloat16),
            pltpu.VMEM((tokens, TILE, HD), jnp.bfloat16),
            pltpu.VMEM((slots * rows, HD), jnp.bfloat16),
            pltpu.VMEM((2, slots * rows, SPAN * TILE), jnp.float32),
            pltpu.VMEM((2, slots * rows, SPAN * TILE), jnp.bfloat16),
            pltpu.VMEM((slots * rows, 128), jnp.float32),
            pltpu.VMEM((slots * rows, HD), jnp.float32),
            pltpu.VMEM((STAGES, slots, rows, HD), jnp.float32),
            pltpu.VMEM((STAGES, slots, rows // 2, HD), jnp.float32),
            pltpu.VMEM((STAGES, slots, rows // 2, HD), jnp.bfloat16),
            pltpu.VMEM((STAGES, tokens, rows // 2, HD), jnp.bfloat16),
            pltpu.VMEM((TILE, inner), jnp.bfloat16),
            pltpu.VMEM((TILE, inner), jnp.bfloat16),
            pltpu.SMEM((tokens,), jnp.int32),
            dma((3,)),
            dma((2,)),
            dma((6, PARTS)),
            dma((images - 1, 2, PARTS)),
            dma((2,)),
            dma((2,)),
            dma((STAGES,)),
            dma((STAGES,)),
            dma((STAGES,)),
            dma((STAGES,)),
            dma,
            dma,
        ],
        compiler_params=pltpu.CompilerParams(
            collective_id=0, has_side_effects=True, vmem_limit_bytes=60 * 1024 * 1024
        ),
    )(masked_tiles, mask_count, guide, hidden, key_cache, value_cache, w_query, cached_out)


def solution(mesh):
    return jax.shard_map(
        body,
        mesh=mesh,
        in_specs=(
            P(None, "image", "token", None),
            P(None, "image", "token", None),
            P(None, "image", "token", None),
            P("image", "token", None),
            P("image", None),
            P("image"),
            P("image", None),
            P("image"),
        ),
        out_specs=P("image", "token", None),
        check_vma=False,
    )
```

```python
import functools
import math

import jax
import jax.numpy as jnp
from jax import lax
from jax.experimental import pallas as pl
from jax.experimental.pallas import tpu as pltpu
from jax.sharding import PartitionSpec as P

HD = 128
TILE = 128
SIDE = 4
STAGES = 4
PARTS = 6
DEPTH = 2
BLOCK = 32
SPAN = 8
MESH = pl.DeviceIdType.MESH
LOG2E = 1.4426950408889634


def head_of(row, col):
    turn = (col - row - 1) & (SIDE - 1)
    last = SIDE - 2
    return row * (SIDE - 1) + jnp.minimum(turn, last), turn <= last


OFFSETS = tuple(
    ((2 * (i // SIDE) + i) % SIDE, (3 * (i // SIDE) + i) % SIDE) for i in range(1, SIDE * SIDE)
)


def kernel(
    tiles_ref,
    count_ref,
    guide_ref,
    hidden_ref,
    key_ref,
    value_ref,
    w_ref,
    cached_ref,
    out_ref,
    hid,
    wbuf,
    acc,
    qsend,
    qbuf,
    qnow,
    kbuf,
    vbuf,
    query,
    score,
    heavy,
    totals,
    sums,
    attended,
    other,
    guided,
    osend,
    arrived,
    cached,
    slot_of,
    local_sem,
    hid_sem,
    w_send,
    w_recv,
    kv_send,
    kv_recv,
    q_send,
    q_recv,
    x_send,
    x_recv,
    o_send,
    o_recv,
):
    image = lax.axis_index("image")
    token = lax.axis_index("token")
    images = hidden_ref.shape[3] // w_ref.shape[0]
    core = token & 1
    chip = token >> 1
    partner = token ^ 1
    row = chip >> 2
    col = chip & (SIDE - 1)
    my_head, has_head = head_of(row, col)
    odd = (row + col) & 1
    right = (row * SIDE + ((col + 1) & (SIDE - 1))) * 2 + core
    left = (row * SIDE + ((col - 1) & (SIDE - 1))) * 2 + core
    below = (((row + 1) & (SIDE - 1)) * SIDE + col) * 2 + core
    above = (((row - 1) & (SIDE - 1)) * SIDE + col) * 2 + core
    token_count = 2 * SIDE * SIDE
    heads = key_ref.shape[3] // HD
    half_heads = heads // 2
    depth = w_ref.shape[0]
    half_cols = w_ref.shape[1] // 2
    slots = tiles_ref.shape[1]
    up = (image + 1) & (images - 1)
    down = (image - 1) & (images - 1)
    far = image ^ 2

    my_cols = pl.ds(pl.multiple_of(core * half_cols, 128), half_cols)
    w_own = pltpu.make_async_copy(w_ref.at[:, my_cols], wbuf.at[0], local_sem.at[0])
    w_own.start()
    hid_own = pltpu.make_async_copy(hidden_ref.at[:, 0], hid.at[:, core], local_sem.at[1])
    hid_own.start()
    cached_own = pltpu.make_async_copy(cached_ref.at[0], cached, local_sem.at[2])
    cached_own.start()

    barrier = pltpu.get_barrier_semaphore()

    for near in (up, down):
        pl.semaphore_signal(barrier, inc=1, device_id=(near, token), device_id_type=MESH)
    for step in range(1, token_count):
        peer = token ^ step
        pl.semaphore_signal(barrier, inc=1, device_id=(image, peer), device_id_type=MESH)
    pl.semaphore_wait(barrier, token_count - 1 + 2)

    half = depth // 2
    piece = half // PARTS
    early_1, early_2 = 1 - odd, odd

    def w_rows(part, k):
        return pl.ds(pl.multiple_of(part * half + k * piece, piece), piece)

    def w_copy(index, src, slot, part, k, to_image, to_token):
        return pltpu.make_async_remote_copy(
            src_ref=src,
            dst_ref=wbuf.at[slot, w_rows(part, k)],
            send_sem=w_send.at[index, k],
            recv_sem=w_recv.at[slot - 1, part, k],
            device_id=(to_image, to_token),
            device_id_type=MESH,
        )

    def w_direct(index, slot, part, k):
        near = up if slot == 1 else down
        return w_copy(index, w_ref.at[w_rows(part, k), my_cols], slot, part, k, near, token)

    def w_pass(index, slot, part, k, new_slot, to_image, to_token):
        src = wbuf.at[slot, w_rows(part, k)]
        return w_copy(index, src, new_slot, part, k, to_image, to_token)

    def w_wait(slot, part, k):
        dst = wbuf.at[slot, w_rows(part, k)]
        pltpu.make_async_copy(dst, dst, w_recv.at[slot - 1, part, k]).wait()

    def direct_early(k):
        return w_direct(0, 1, early_1, k), w_direct(1, 2, early_2, k)

    def direct_late(k):
        return w_direct(2, 1, 0, k), w_direct(3, 2, 1, k)

    def near_pair(k):
        return (right, left) if k % 2 == 0 else (below, above)

    def pass_early(k):
        near_1, near_2 = near_pair(k)
        to_1 = jnp.where(odd == 1, token, near_1)
        to_2 = jnp.where(odd == 1, token, near_2)
        return (
            w_pass(4, 1, early_1, k, 1 + 2 * odd, jnp.where(odd == 1, up, image), to_1),
            w_pass(5, 2, early_2, k, 2 + odd, jnp.where(odd == 1, down, image), to_2),
        )

    def pass_late(k):
        near_1, near_2 = near_pair(k)
        return w_pass(2, 3, 0, k, 3, image, near_1), w_pass(3, 3, 1, k, 3, image, near_2)

    for k in range(PARTS):
        for copy in direct_early(k):
            copy.start()

    hid_out = pltpu.make_async_remote_copy(
        src_ref=hidden_ref.at[:, 0],
        dst_ref=hid.at[:, core],
        send_sem=hid_sem.at[0],
        recv_sem=hid_sem.at[1],
        device_id=(image, partner),
        device_id_type=MESH,
    )
    hid_out.start()

    def kv_pairs(head, branch):
        lanes = pl.ds(pl.multiple_of(head * HD, HD), HD)
        return (
            (key_ref.at[branch, 0, :, lanes], kbuf.at[token], 0),
            (value_ref.at[branch, 0, :, lanes], vbuf.at[token], 1),
        )

    def kv_start(head, branch, target):
        for src, dst, kind in kv_pairs(head, branch):
            pltpu.make_async_remote_copy(
                src_ref=src,
                dst_ref=dst,
                send_sem=kv_send.at[kind],
                recv_sem=kv_recv.at[kind],
                device_id=(image, target),
                device_id_type=MESH,
            ).start()

    for down_rows, right_cols in OFFSETS:
        to_row, to_col = (row + down_rows) & (SIDE - 1), (col + right_cols) & (SIDE - 1)
        to_head, there = head_of(to_row, to_col)
        to_chip = to_row * SIDE + to_col

        @pl.when(there)
        def _():
            for branch in range(2):
                kv_start(to_head, branch, to_chip * 2 + branch)

    @pl.when(has_head)
    def _():
        kv_start(my_head, 1 - core, partner)
        for src, dst, kind in kv_pairs(my_head, core):
            pltpu.make_async_copy(src, dst, kv_recv.at[kind]).start()

    @pl.when(odd == 0)
    def _():
        for k in range(PARTS):
            for copy in direct_late(k):
                copy.start()

    @pl.loop(0, token_count)
    def _(tile):
        slot = jnp.int32(0)
        for j in range(slots):
            hit = (tiles_ref[0, j] == tile) & (count_ref[0] > j)
            slot = jnp.where(hit, jnp.int32(j), slot)
        slot_of[tile] = slot

    rows_all = 4 * TILE
    width = 256

    def project(slot, owner, start, size, is_first):
        features = pl.ds(pl.multiple_of(owner * depth + start, 128), size)
        w_part = pl.ds(pl.multiple_of(start, 128), size)

        @pl.loop(0, half_cols // width)
        def _(step):
            cols = pl.ds(pl.multiple_of(step * width, width), width)
            part = jnp.dot(
                hid[:, :, :, features].reshape(rows_all, size),
                wbuf[slot, w_part, cols],
                preferred_element_type=jnp.float32,
            ).reshape(2, 2, TILE, width)
            if is_first:
                acc[:, :, :, cols] = part
            else:
                acc[:, :, :, cols] += part

    w_own.wait()
    hid_own.wait()
    hid_out.wait_recv()
    project(0, image, 0, depth, True)
    for k in range(PARTS):
        first, second = pass_early(k)
        w_wait(1, early_1, k)
        first.start()
        w_wait(2, early_2, k)
        second.start()
    project(1, down, early_1 * half, half, False)
    project(2, up, early_2 * half, half, False)

    @pl.when(odd == 1)
    def _():
        for k in range(PARTS):
            first, second = pass_late(k)
            w_wait(3, 0, k)
            first.start()
            w_wait(3, 1, k)
            second.start()

    for k in range(PARTS):
        w_wait(1, 1 - early_1, k)
    project(1, down, (1 - early_1) * half, half, False)
    for k in range(PARTS):
        w_wait(2, 1 - early_2, k)
    project(2, up, (1 - early_2) * half, half, False)

    @pl.when(odd == 0)
    def _():
        for k in range(PARTS):
            w_wait(3, 0, k)
            w_wait(3, 1, k)

    project(3, far, 0, depth, False)

    rows = TILE // STAGES

    def q_start(stage, head, branch, target):
        pltpu.make_async_remote_copy(
            src_ref=qsend.at[stage, branch, head - core * half_heads],
            dst_ref=qbuf.at[stage, pl.ds(chip * 2, 2)],
            send_sem=q_send.at[stage],
            recv_sem=q_recv.at[stage],
            device_id=(image, target),
            device_id_type=MESH,
        ).start()

    def sent(ref, sem):
        pltpu.make_async_copy(ref, ref, sem).wait()

    owns_head = has_head & (row >> 1 == core)

    def q_sent(stage):
        @pl.when(owns_head)
        def _():
            sent(qbuf.at[stage, pl.ds(0, 4 * half_heads - 2)], q_send.at[stage])

        @pl.when(jnp.logical_not(owns_head))
        def _():
            sent(qbuf.at[stage, pl.ds(0, 4 * half_heads)], q_send.at[stage])

    for stage in range(STAGES):
        for head in range(half_heads):
            block = acc[:, :, stage * rows : (stage + 1) * rows, head * HD : (head + 1) * HD]
            qsend[stage, :, head] = block.astype(jnp.bfloat16)
        if stage >= DEPTH:
            q_sent(stage - DEPTH)

        for step in range(2 * SIDE):
            to_row = 2 * core + ((row + step) & 1)
            to_col = (col + step + step // SIDE) & (SIDE - 1)
            to_head, there = head_of(to_row, to_col)
            to_chip = to_row * SIDE + to_col

            @pl.when(there & (to_chip != chip))
            def _():
                for branch in range(2):
                    q_start(stage, to_head, branch, to_chip * 2 + branch)

        @pl.when(owns_head)
        def _():
            q_start(stage, my_head, 1 - core, partner)
            pltpu.make_async_copy(
                qsend.at[stage, core, my_head - core * half_heads],
                qbuf.at[stage, pl.ds(chip * 2, 2)],
                q_recv.at[stage],
            ).start()

    share = rows // 2
    mine_rows = pl.ds(pl.multiple_of(core * share, share), share)
    sent_rows = pl.ds(pl.multiple_of((1 - core) * share, share), share)
    factor = LOG2E / math.sqrt(HD)
    span = SPAN
    chunk = span * TILE
    chunks = token_count // span
    height = slots * rows

    def exchange(stage):
        return pltpu.make_async_remote_copy(
            src_ref=attended.at[stage, :, sent_rows],
            dst_ref=other.at[stage],
            send_sem=x_send.at[stage],
            recv_sem=x_recv.at[stage],
            device_id=(image, partner),
            device_id_type=MESH,
        )

    def o_refs(stage, target):
        lanes = pl.ds(pl.multiple_of(my_head * HD, HD), HD)
        put = pl.ds(pl.multiple_of(stage * rows + core * share, share), share)
        return osend.at[stage, target], arrived.at[put, lanes]

    def o_start(stage, target):
        src, dst = o_refs(stage, target)
        pltpu.make_async_remote_copy(
            src_ref=src,
            dst_ref=dst,
            send_sem=o_send,
            recv_sem=o_recv,
            device_id=(image, target),
            device_id_type=MESH,
        ).start()

    def attention(stage):
        qnow[...] = qbuf[stage]
        for j in range(slots):
            query[j * rows : (j + 1) * rows] = qnow[tiles_ref[0, j]]

        def logits(part):
            keys = kbuf[part * span : (part + 1) * span].reshape(chunk, HD)
            score[part % 2] = lax.dot_general(
                query[...], keys, (((1,), (1,)), ((), ())), preferred_element_type=jnp.float32
            )

        blocks = range(0, height, BLOCK)
        top = [None for _ in blocks]
        logits(0)
        for part in range(chunks):
            if part + 1 < chunks:
                logits(part + 1)
            shrink = []
            for index, low in enumerate(blocks):
                some = pl.ds(low, BLOCK)
                peak = score[part % 2, some, 0:128]
                for lane in range(1, span):
                    peak = jnp.maximum(peak, score[part % 2, some, lane * 128 : (lane + 1) * 128])
                peak = jnp.max(peak, axis=-1, keepdims=True) * factor
                if part > 0:
                    peak = jnp.maximum(peak, top[index])
                    shrink.append(jnp.exp2(top[index] - peak))
                top[index] = peak
                total = None
                for lane in range(span):
                    lanes = slice(lane * 128, (lane + 1) * 128)
                    weight = jnp.exp2(score[part % 2, some, lanes] * factor - peak)
                    heavy[part % 2, some, lanes] = weight.astype(jnp.bfloat16)
                    total = weight if total is None else total + weight
                if part > 0:
                    total = total + totals[some] * shrink[index]
                totals[some] = total
            values = vbuf[part * span : (part + 1) * span].reshape(chunk, HD)
            summed = jnp.dot(heavy[part % 2], values, preferred_element_type=jnp.float32)
            for index, low in enumerate(blocks):
                some = pl.ds(low, BLOCK)
                block = summed[low : low + BLOCK]
                if part > 0:
                    block = block + sums[some] * shrink[index]
                sums[some] = block
        done = sums[...] / jnp.sum(totals[...], axis=-1, keepdims=True)
        attended[stage] = done.reshape(slots, rows, HD)

    def deliver(stage):
        exchange(stage).wait_recv()
        scale = guide_ref[0]
        mine = attended[stage, :, mine_rows]
        theirs = other[stage]
        cond = jnp.where(core == 0, mine, theirs)
        uncond = jnp.where(core == 0, theirs, mine)
        guided[stage] = (uncond + scale * (cond - uncond)).astype(jnp.bfloat16)

        for tile in range(token_count):
            osend[stage, tile] = guided[stage, slot_of[tile]]

        for down_rows, right_cols in OFFSETS:
            to_row, to_col = (row + down_rows) & (SIDE - 1), (col + right_cols) & (SIDE - 1)
            for to_core in range(2):
                o_start(stage, (to_row * SIDE + to_col) * 2 + to_core)
        o_start(stage, partner)
        src, dst = o_refs(stage, token)
        pltpu.make_async_copy(src, dst, o_recv).start()

    @pl.when(has_head)
    def _():
        pltpu.make_async_copy(kbuf, kbuf, kv_recv.at[0]).wait()
        pltpu.make_async_copy(vbuf, vbuf, kv_recv.at[1]).wait()

        @pl.loop(0, STAGES + 1)
        def _(stage):
            @pl.when(stage < STAGES)
            def _():
                pltpu.make_async_copy(qbuf.at[stage], qbuf.at[stage], q_recv.at[stage]).wait()
                attention(stage)
                exchange(stage).start()

            @pl.when(stage > 0)
            def _():
                deliver(stage - 1)

    hid_out.wait_send()
    for k in range(PARTS):
        for copy in direct_early(k) + pass_early(k):
            copy.wait_send()

    @pl.when(odd == 0)
    def _():
        for k in range(PARTS):
            for copy in direct_late(k):
                copy.wait_send()

    @pl.when(odd == 1)
    def _():
        for k in range(PARTS):
            for copy in pass_late(k):
                copy.wait_send()

    @pl.when(has_head)
    def _():
        sent(kbuf.at[pl.ds(0, 2 * heads - 1)], kv_send.at[0])
        sent(vbuf.at[pl.ds(0, 2 * heads - 1)], kv_send.at[1])
        sent(osend.at[:, pl.ds(0, token_count - 1)], o_send)
        for stage in range(STAGES):
            exchange(stage).wait_send()

    @pl.when(jnp.logical_not(has_head))
    def _():
        sent(kbuf.at[pl.ds(0, 2 * heads)], kv_send.at[0])
        sent(vbuf.at[pl.ds(0, 2 * heads)], kv_send.at[1])

    for stage in range(STAGES - DEPTH, STAGES):
        q_sent(stage)

    pasted = jnp.int32(0)
    for j in range(slots):
        hit = (tiles_ref[0, j] == token) & (count_ref[0] > j)
        pasted = jnp.where(hit, jnp.int32(1), pasted)
    cached_own.wait()
    pltpu.make_async_copy(arrived, arrived, o_recv).wait()
    out_ref[0] = jnp.where(pasted == 1, arrived[...], cached[...])


def body(hidden, key_cache, value_cache, cached_out, w_query, guide, masked_tiles, mask_count):
    tokens = 2 * SIDE * SIDE
    inner = key_cache.shape[3]
    heads = inner // HD
    slots = masked_tiles.shape[1]
    width = hidden.shape[3]
    images = width // w_query.shape[0]
    rows = TILE // STAGES
    dma = pltpu.SemaphoreType.DMA
    return pl.pallas_call(
        kernel,
        out_shape=pltpu.VMEM((1, TILE, inner), jnp.bfloat16),
        in_specs=[pl.BlockSpec(memory_space=pltpu.SMEM)] * 3
        + [pl.BlockSpec(memory_space=pl.ANY)] * 5,
        out_specs=pl.BlockSpec(memory_space=pltpu.VMEM),
        scratch_shapes=[
            pltpu.VMEM((2, 2, TILE, width), jnp.bfloat16),
            pltpu.VMEM((images, w_query.shape[0], inner // 2), jnp.bfloat16),
            pltpu.VMEM((2, 2, TILE, inner // 2), jnp.float32),
            pltpu.VMEM((STAGES, 2, heads // 2, 2, rows, HD), jnp.bfloat16),
            pltpu.VMEM((STAGES, tokens, rows, HD), jnp.bfloat16),
            pltpu.VMEM((tokens, rows, HD), jnp.bfloat16),
            pltpu.VMEM((tokens, TILE, HD), jnp.bfloat16),
            pltpu.VMEM((tokens, TILE, HD), jnp.bfloat16),
            pltpu.VMEM((slots * rows, HD), jnp.bfloat16),
            pltpu.VMEM((2, slots * rows, SPAN * TILE), jnp.float32),
            pltpu.VMEM((2, slots * rows, SPAN * TILE), jnp.bfloat16),
            pltpu.VMEM((slots * rows, 128), jnp.float32),
            pltpu.VMEM((slots * rows, HD), jnp.float32),
            pltpu.VMEM((STAGES, slots, rows, HD), jnp.float32),
            pltpu.VMEM((STAGES, slots, rows // 2, HD), jnp.float32),
            pltpu.VMEM((STAGES, slots, rows // 2, HD), jnp.bfloat16),
            pltpu.VMEM((STAGES, tokens, rows // 2, HD), jnp.bfloat16),
            pltpu.VMEM((TILE, inner), jnp.bfloat16),
            pltpu.VMEM((TILE, inner), jnp.bfloat16),
            pltpu.SMEM((tokens,), jnp.int32),
            dma((3,)),
            dma((2,)),
            dma((6, PARTS)),
            dma((images - 1, 2, PARTS)),
            dma((2,)),
            dma((2,)),
            dma((STAGES,)),
            dma((STAGES,)),
            dma((STAGES,)),
            dma((STAGES,)),
            dma,
            dma,
        ],
        compiler_params=pltpu.CompilerParams(
            collective_id=0, has_side_effects=True, vmem_limit_bytes=60 * 1024 * 1024
        ),
    )(masked_tiles, mask_count, guide, hidden, key_cache, value_cache, w_query, cached_out)


def solution(mesh):
    return jax.shard_map(
        body,
        mesh=mesh,
        in_specs=(
            P(None, "image", "token", None),
            P(None, "image", "token", None),
            P(None, "image", "token", None),
            P("image", "token", None),
            P("image", None),
            P("image"),
            P("image", None),
            P("image"),
        ),
        out_specs=P("image", "token", None),
        check_vma=False,
    )
```
